32 devices in a mesh: vp: 4 (over y, x), cp: 2 (over core), ga: 4 (over z).
Axes of the slice: x: 2, y: 2, z: 4, core: 2. Of those that a mesh axis runs over, the one named last changes fastest.
Arguments:
- valence_wavefunction: bfloat16 [512, 24576], P(('vp', 'cp'), 'ga'), may hold values from -6 to 6
- cond_wave: bfloat16 [512, 24576], P(('vp', 'cp'), 'ga'), may hold values from -6 to 6
- screen_basis: bfloat16 [24576, 1024], P('ga'), may hold values from -0.0390625 to 0.0390625
- screen: float32 [1024], replicated, may hold values from 0.01 to 0.1
- coulomb: float32 [1024], replicated, may hold values from 0.02 to 0.2
- window_rows: int32 [2], replicated, may hold values from 0 to 1023
- tile_owner: int32 [48], P(('vp', 'cp')), may hold values from 0 to 4095, as said below
Outputs:
- kernel: float32 [2, 48, 4096], P(None, ('vp', 'cp'), 'ga')
The draws below stay inside these ranges and needn't reach their ends.
Inputs may be any that keep to these rules, and one draw needn't show every extreme that they name: `tile_owner`: distinct pair-block indices; 0 and 4095 both occur.
All inputs are finite; a program needn't handle non-finite values.
Results may differ from the reference program's by a relative error of at most 0.02.
Values may be sent and summed in bfloat16 or wider, within the bound.
A program may use at most 64 MiB of HBM per device.

```python
import math
import jax
import jax.numpy as jnp
from jax import lax

NV = 512
NC = 512
NG = 24576
R = 1024
TV = 8
TC = 8
G_DEV = 6144
NCT = 64
PAIR_BLOCK_COUNT = 4096
WINDOW_TILE_COUNT = 48
N_GA = 4


def draw_tile_owner(key, part):
    middle_factor = jax.random.permutation(jax.random.fold_in(key, 11), PAIR_BLOCK_COUNT - 2)[:WINDOW_TILE_COUNT - 2].astype(jnp.int32) + 1
    values = jnp.concatenate([jnp.array([0, PAIR_BLOCK_COUNT - 1], jnp.int32), middle_factor])
    band_order = jax.random.permutation(jax.random.fold_in(key, 12), WINDOW_TILE_COUNT)
    return values[band_order]


def shard_levels(own_key, dims, shards, smallest, largest):
    def one(axis_at, blocks):
        heights = jax.random.uniform(jax.random.fold_in(jax.random.fold_in(own_key, 6), axis_at), (blocks,), jnp.float32, smallest / len(shards), largest / len(shards))
        return jnp.repeat(jnp.exp(heights), dims[axis_at] // blocks).reshape((-1,) + (1,) * (len(dims) - axis_at - 1))

    level = one(*shards[0])
    for cut in shards[1:]:
        level = level * one(*cut)
    return level


def noise(own_key, shape, spread, reach, shards=(), dtype=jnp.bfloat16):
    drawn = spread * jax.random.normal(own_key, shape, jnp.float32)
    if shards:
        drawn = drawn * shard_levels(own_key, shape, shards, -0.22, 0.18)
    return jnp.clip(drawn, -reach, reach).astype(dtype)


def setup_inputs(seed: int = 0) -> dict:
    streams_of = jax.random.split(jax.random.key(seed), 8)
    return {
        "valence_wavefunction": noise(streams_of[0], (NV, NG), 1.0, 6.0, ((0, 8), (1, 4))),
        "cond_wave": noise(streams_of[1], (NC, NG), 1.0, 6.0, ((0, 8), (1, 4))),
        "screen_basis": noise(streams_of[2], (NG, R), NG ** -0.5, 0.0390625, ((0, 4),)),
        "screen": jnp.clip(jnp.exp(jax.random.uniform(streams_of[3], (R,), jnp.float32, math.log(0.01), math.log(0.1))), 0.01, 0.1),
        "coulomb": jnp.clip(jnp.exp(jax.random.uniform(streams_of[4], (R,), jnp.float32, math.log(0.02), math.log(0.2))), 0.02, 0.2),
        "window_rows": jax.random.randint(streams_of[5], (2,), 0, PAIR_BLOCK_COUNT // 4).astype(jnp.int32),
        "tile_owner": draw_tile_owner(jax.random.fold_in(streams_of[7], 71), 0),
    }


def band_block(wave, tile_index, span):
    return lax.dynamic_slice_in_dim(wave, (tile_index * span).astype(jnp.int32), span, 0)


def pair_rows(left_wavefunction, right_wave):
    product = left_wavefunction.astype(jnp.float32)[:, None, :] * right_wave.astype(jnp.float32)[None, :, :]
    return product.reshape(-1, left_wavefunction.shape[1]).astype(jnp.bfloat16)


def project(rho, blocks):
    parts = rho.astype(jnp.float32).reshape(rho.shape[0], N_GA, G_DEV)
    partial_value = jnp.einsum("pkg,kgr->kpr", parts, blocks)
    rounded = lax.optimization_barrier(partial_value.astype(jnp.bfloat16))
    return jnp.sum(rounded.astype(jnp.float32), axis=0)


def reference(valence_wavefunction, cond_wave, screen_basis, screen, coulomb, window_rows, tile_owner):
    blocks = screen_basis.astype(jnp.float32).reshape(N_GA, G_DEV, R)
    row_val = [band_block(valence_wavefunction, window_rows[window_row] // NCT, TV) for window_row in range(2)]
    row_cond = [band_block(cond_wave, window_rows[window_row] % NCT, TC) for window_row in range(2)]
    row_proj = [project(pair_rows(row_val[window_row], row_cond[window_row]), blocks) for window_row in range(2)]

    def per_slot(owner_index):
        slot_valence = band_block(valence_wavefunction, owner_index // NCT, TV)
        slot_cond = band_block(cond_wave, owner_index % NCT, TC)
        col_proj = project(pair_rows(slot_valence, slot_cond), blocks)
        results = []
        for window_row in range(2):
            val_proj = project(pair_rows(row_val[window_row], slot_valence), blocks).reshape(TV, TV, R)
            cond_proj = project(pair_rows(row_cond[window_row], slot_cond), blocks).reshape(TC, TC, R)
            exchange_term = jnp.dot(row_proj[window_row] * coulomb[None, :], col_proj.T, precision=lax.Precision.HIGHEST)
            direct_term = jnp.einsum("vwr,cdr->vcwd", val_proj * screen, cond_proj, precision=lax.Precision.HIGHEST)
            total = 2.0 * exchange_term - direct_term.reshape(TV * TC, TV * TC)
            live_tile = owner_index >= window_rows[window_row]
            results.append(jnp.where(live_tile, total, jnp.zeros_like(total)).reshape(-1))
        return jnp.stack(results)

    stacked = lax.map(per_slot, tile_owner)
    return jnp.transpose(stacked, (1, 0, 2))
```

```python
import functools
import jax
import jax.numpy as jnp
from jax import lax
from jax.experimental import pallas as pl
from jax.experimental.pallas import tpu as pltpu
from jax.sharding import PartitionSpec as P

TV = 8
TC = 8
NCT = 64
LAG = 2
ROW_TILES = 2


def select_bands(wanted, shard_part):
    row_ids = jnp.arange(shard_part.shape[0], dtype=jnp.int32)
    chooser = (wanted[:, None] == row_ids[None, :]).astype(jnp.bfloat16)
    return jnp.dot(chooser, shard_part, preferred_element_type=jnp.float32)


def pair_rows(rho, first, left, right, lanes):
    for i in range(len(left)):
        rho[pl.ds(first + 16 * i, 16), lanes] = left[i] * right


def spread(tile):
    out = []
    for i in range(0, tile.shape[0], 2):
        two = [jnp.broadcast_to(tile[i + j : i + j + 1], (8, tile.shape[1])) for j in range(2)]
        out.append(jnp.concatenate(two, axis=0).astype(jnp.bfloat16))
    return out


def twice(tile):
    return jnp.concatenate([tile, tile], axis=0).astype(jnp.bfloat16)


def dot_t(a, b):
    return lax.dot_general(a, b, (((1,), (1,)), ((), ())), preferred_element_type=jnp.float32)


def weighted_dot(a, weight, b):
    scaled = a.astype(jnp.float32) * weight
    high = scaled.astype(jnp.bfloat16)
    low = (scaled - high.astype(jnp.float32)).astype(jnp.bfloat16)
    return dot_t(high, b) + dot_t(low, b)


def tiles_kernel(
    n, slots, val_ref, cond_ref, basis_hbm, screen_ref, coulomb_ref, exch_ref, direct_ref,
    basis, rho, acc, own, got, ex_own, dr_own, ex_send, dr_send, ex_got, dr_got,
    basis_sem, send_sem, recv_sem, fin_send, fin_recv,
):
    z = lax.axis_index("ga")
    grid, rank = basis_hbm.shape
    steps, rows, width = own.shape[1:]
    halves = rank // (2 * width)
    ends = (0, n - 1)
    block = TV * TC

    copies = []
    for c in range(2 * halves):
        cols = pl.ds(c * width, width)
        copy = pltpu.make_async_copy(basis_hbm.at[:, cols], basis.at[:, cols], basis_sem.at[c])
        copy.start()
        copies.append(copy)

    barrier = pltpu.get_barrier_semaphore()
    for other in range(1, n):
        pl.semaphore_signal(
            barrier, inc=1, device_id={"ga": lax.rem(z + other, n)}, device_id_type=pl.DeviceIdType.MESH
        )

    lane = 256

    def densities(g, _):
        lanes = pl.ds(pl.multiple_of(g * lane, lane), lane)
        val = val_ref[:, lanes].astype(jnp.float32)
        cond = cond_ref[:, lanes].astype(jnp.float32)
        row_val = [spread(val[q * TV : (q + 1) * TV]) for q in range(ROW_TILES)]
        row_cond = [spread(cond[q * TC : (q + 1) * TC]) for q in range(ROW_TILES)]
        for q in range(ROW_TILES):
            pair_rows(rho, q * block, row_val[q], twice(cond[q * TC : (q + 1) * TC]), lanes)
        for s in range(slots):
            at = (ROW_TILES + s) * 8
            slot_val, slot_cond = val[at : at + TV], cond[at : at + TC]
            right_val, right_cond = twice(slot_val), twice(slot_cond)
            pair_rows(rho, (ROW_TILES + s) * block, spread(slot_val), right_cond, lanes)
            first = (ROW_TILES + slots + 2 * ROW_TILES * s) * block
            for q in range(ROW_TILES):
                pair_rows(rho, first + q * block, row_val[q], right_val, lanes)
                pair_rows(rho, first + (ROW_TILES + q) * block, row_cond[q], right_cond, lanes)
        return 0

    lax.fori_loop(0, grid // lane, densities, 0)
    pl.semaphore_wait(barrier, n - 1)

    depth = 1024
    toward = (-1, 1)

    def hop(way, k):
        return pltpu.make_async_remote_copy(
            src_ref=own.at[way, k],
            dst_ref=got.at[way, k],
            send_sem=send_sem.at[way, k],
            recv_sem=recv_sem.at[way, k],
            device_id={"ga": lax.rem(z + toward[way] + n, n)},
            device_id_type=pl.DeviceIdType.MESH,
        )

    far = (n - 1 - z, z)

    def step(i, _):
        @pl.when(i < steps)
        def _():
            first = pl.multiple_of((i // halves) * rows, rows)
            for way in range(2):
                part = way * halves + lax.rem(i, halves)
                column = pl.multiple_of(part * width, width)

                for c in range(halves):
                    @pl.when(i == c)
                    def _():
                        copies[way * halves + c].wait()

                acc[...] = jnp.zeros_like(acc)

                def deep(k, _):
                    at = pl.multiple_of(k * depth, depth)
                    acc[...] += jnp.dot(
                        rho[pl.ds(first, rows), pl.ds(at, depth)],
                        basis[pl.ds(at, depth), pl.ds(column, width)],
                        preferred_element_type=jnp.float32,
                    )
                    return 0

                lax.fori_loop(0, grid // depth, deep, 0)
                own[way, i] = acc[...].astype(jnp.bfloat16)

        for way in range(2):
            k = i - LAG * far[way]

            @pl.when(jnp.logical_and(k >= 0, k < steps))
            def _():
                @pl.when(far[way] > 0)
                def _():
                    hop(way, k).wait_recv()
                    total = own[way, k].astype(jnp.float32) + got[way, k].astype(jnp.float32)
                    own[way, k] = total.astype(jnp.bfloat16)

                @pl.when(z != ends[way])
                def _():
                    hop(way, k).start()

        return 0

    lax.fori_loop(0, steps + LAG * (n - 1), step, 0)

    share = block // n

    def give(way, k):
        return [
            pltpu.make_async_remote_copy(
                src_ref=sent.at[k],
                dst_ref=there.at[way],
                send_sem=fin_send.at[k, j],
                recv_sem=fin_recv.at[way, j],
                device_id={"ga": k},
                device_id_type=pl.DeviceIdType.MESH,
            )
            for j, (sent, there) in enumerate(((ex_send, ex_got), (dr_send, dr_got)))
        ]

    for way in range(2):
        @pl.when(z == ends[way])
        def _():
            exchange = jnp.zeros(ex_own.shape, jnp.float32)
            for c in range(halves):
                weight = coulomb_ref[:, pl.ds((way * halves + c) * width, width)]
                left = own[way, c, pl.ds(0, ROW_TILES * block), :]
                right = own[way, c, pl.ds(ROW_TILES * block, slots * block), :]
                exchange += weighted_dot(left, weight, right)
            ex_own[...] = exchange
            wide = ROW_TILES * block
            for s in range(slots):
                first = (ROW_TILES + slots + 2 * ROW_TILES * s) * block
                job, at = first // rows, first % rows
                direct = jnp.zeros((wide, wide), jnp.float32)
                for c in range(halves):
                    weight = screen_ref[:, pl.ds((way * halves + c) * width, width)]
                    left = own[way, job * halves + c, pl.ds(at, wide), :]
                    right = own[way, job * halves + c, pl.ds(at + wide, wide), :]
                    direct += weighted_dot(left, weight, right)
                column = lax.broadcasted_iota(jnp.int32, (block, wide), 1)
                dr_own[s] = jnp.where(column < block, direct[:block], direct[block:])
            for k in range(n):
                if k != ends[way]:
                    for q in range(ROW_TILES):
                        ex_send[k, q] = ex_own[pl.ds(q * block + k * share, share), :].astype(jnp.bfloat16)
                    dr_send[k] = dr_own[:, pl.ds(k * share, share), :].astype(jnp.bfloat16)
                    for copy in give(way, k):
                        copy.start()
            for q in range(ROW_TILES):
                exch_ref[q] = ex_own[pl.ds(q * block + ends[way] * share, share), :]
            direct_ref[...] = dr_own[:, pl.ds(ends[way] * share, share), :]

    for way in range(2):
        @pl.when(z != ends[way])
        def _():
            for copy in give(way, 0):
                copy.wait_recv()
            here = ends[1 - way]

            def put(fresh):
                ex_part = ex_got[way].astype(jnp.float32)
                dr_part = dr_got[way].astype(jnp.float32)
                exch_ref[...] = ex_part if fresh else exch_ref[...] + ex_part
                direct_ref[...] = dr_part if fresh else direct_ref[...] + dr_part

            if way == 0:
                pl.when(z == here)(lambda: put(False))
                pl.when(z != here)(lambda: put(True))
            else:
                put(False)

    for way in range(2):
        @pl.when(z != ends[way])
        def _():
            def drain(k, _):
                hop(way, k).wait_send()
                return 0

            lax.fori_loop(0, steps, drain, 0)

        @pl.when(z == ends[way])
        def _():
            for k in range(n):
                if k != ends[way]:
                    for copy in give(way, k):
                        copy.wait_send()


def make_tiles(n, slots, val, cond, basis, screen, coulomb):
    grid, rank = basis.shape
    width = rank // 4
    block = TV * TC
    rows = (ROW_TILES + slots) * block
    total = (ROW_TILES + slots + 2 * ROW_TILES * slots) * block
    steps = (total // rows) * 2
    share = block // n
    vmem = pl.BlockSpec(memory_space=pltpu.VMEM)
    bf16, f32 = jnp.bfloat16, jnp.float32
    return pl.pallas_call(
        functools.partial(tiles_kernel, n, slots),
        out_shape=(
            jax.ShapeDtypeStruct((ROW_TILES, share, slots * block), f32),
            jax.ShapeDtypeStruct((slots, share, ROW_TILES * block), f32),
        ),
        in_specs=[vmem, vmem, pl.BlockSpec(memory_space=pl.ANY), vmem, vmem],
        out_specs=(vmem, vmem),
        scratch_shapes=[
            pltpu.VMEM((grid, rank), bf16),
            pltpu.VMEM((total, grid), bf16),
            pltpu.VMEM((rows, width), f32),
            pltpu.VMEM((2, steps, rows, width), bf16),
            pltpu.VMEM((2, steps, rows, width), bf16),
            pltpu.VMEM((ROW_TILES * block, slots * block), f32),
            pltpu.VMEM((slots, block, ROW_TILES * block), f32),
            pltpu.VMEM((n, ROW_TILES, share, slots * block), bf16),
            pltpu.VMEM((n, slots, share, ROW_TILES * block), bf16),
            pltpu.VMEM((2, ROW_TILES, share, slots * block), bf16),
            pltpu.VMEM((2, slots, share, ROW_TILES * block), bf16),
            pltpu.SemaphoreType.DMA((4,)),
            pltpu.SemaphoreType.DMA((2, steps)),
            pltpu.SemaphoreType.DMA((2, steps)),
            pltpu.SemaphoreType.DMA((n, 2)),
            pltpu.SemaphoreType.DMA((2, 2)),
        ],
        compiler_params=pltpu.CompilerParams(
            collective_id=0, has_side_effects=True, vmem_limit_bytes=67043328
        ),
    )(val, cond, basis, screen, coulomb)


def shards(valence_wavefunction, cond_wave, screen_basis, screen, coulomb, window_rows, tile_owner):
    slots = tile_owner.shape[0]
    n = lax.axis_size("ga")
    pair_tiles = jnp.concatenate([window_rows, tile_owner])
    val_wanted = (
        (pair_tiles // NCT)[:, None] * TV + jnp.arange(TV, dtype=jnp.int32)[None, :]
    ).reshape(-1)
    cond_wanted = (
        (pair_tiles % NCT)[:, None] * TC + jnp.arange(TC, dtype=jnp.int32)[None, :]
    ).reshape(-1)
    val = select_bands(
        val_wanted, lax.all_gather(valence_wavefunction, ("vp", "cp"), axis=0, tiled=True)
    ).astype(jnp.bfloat16)
    cond = select_bands(
        cond_wanted, lax.all_gather(cond_wave, ("vp", "cp"), axis=0, tiled=True)
    ).astype(jnp.bfloat16)
    exchange, direct = make_tiles(n, slots, val, cond, screen_basis, screen[None], coulomb[None])
    v = TV // n
    exchange = exchange.reshape(2, v, TC, slots, TV, TC).transpose(0, 3, 1, 2, 4, 5)
    direct = direct.reshape(slots, v, TV, 2, TC, TC).transpose(3, 0, 1, 4, 2, 5)
    kernel = (2.0 * exchange - direct).reshape(2, slots, -1)
    live = (tile_owner[None, :] >= window_rows[:, None])[:, :, None]
    return jnp.where(live, kernel, jnp.zeros_like(kernel))


def solution(mesh):
    in_specs = (
        P(("vp", "cp"), "ga"),
        P(("vp", "cp"), "ga"),
        P("ga", None),
        P(),
        P(),
        P(),
        P(("vp", "cp")),
    )
    out_specs = P(None, ("vp", "cp"), "ga")
    return jax.shard_map(shards, mesh=mesh, in_specs=in_specs, out_specs=out_specs, check_vma=False)
```

```python
import functools
import jax
import jax.numpy as jnp
from jax import lax
from jax.experimental import pallas as pl
from jax.experimental.pallas import tpu as pltpu
from jax.sharding import PartitionSpec as P

TV = 8
TC = 8
NCT = 64
LAG = 2
ROW_TILES = 2


def pair_rows(rho, first, left, right, lanes):
    for i in range(len(left)):
        rho[pl.ds(first + 16 * i, 16), lanes] = left[i] * right


def spread(tile):
    out = []
    for i in range(0, tile.shape[0], 2):
        two = [jnp.broadcast_to(tile[i + j : i + j + 1], (8, tile.shape[1])) for j in range(2)]
        out.append(jnp.concatenate(two, axis=0).astype(jnp.bfloat16))
    return out


def twice(tile):
    return jnp.concatenate([tile, tile], axis=0).astype(jnp.bfloat16)


def dot_t(a, b):
    return lax.dot_general(a, b, (((1,), (1,)), ((), ())), preferred_element_type=jnp.float32)


def weighted_dot(a, weight, b):
    scaled = a.astype(jnp.float32) * weight
    high = scaled.astype(jnp.bfloat16)
    low = (scaled - high.astype(jnp.float32)).astype(jnp.bfloat16)
    return dot_t(high, b) + dot_t(low, b)


def tiles_kernel(
    n, n_vp, n_cp, slots, val_hbm, cond_hbm, wanted_ref, basis_hbm, screen_ref, coulomb_ref,
    exch_ref, direct_ref, wanted, near, picked, sent, came, total, ready, basis, rho, acc, own, got, ex_own, dr_own, ex_send, dr_send, ex_got, dr_got,
    want_send, want_recv, near_send, near_recv, cross_send, cross_recv, give_send, give_recv,
    basis_sem, send_sem, recv_sem, fin_send, fin_recv,
):
    z = lax.axis_index("ga")
    grid, rank = basis_hbm.shape
    steps, rows, width = own.shape[1:]
    halves = rank // (2 * width)
    ends = (0, n - 1)
    block = TV * TC

    copies = []
    for c in range(2 * halves):
        cols = pl.ds(c * width, width)
        copy = pltpu.make_async_copy(basis_hbm.at[:, cols], basis.at[:, cols], basis_sem.at[c])
        copy.start()
        copies.append(copy)

    barrier = pltpu.get_barrier_semaphore()
    for other in range(1, n):
        pl.semaphore_signal(
            barrier, inc=1, device_id={"ga": lax.rem(z + other, n)}, device_id_type=pl.DeviceIdType.MESH
        )

    vp, cp = lax.axis_index("vp"), lax.axis_index("cp")
    group = n_vp * n_cp
    me = vp * n_cp + cp
    for other in range(1, group):
        peer = lax.rem(me + other, group)
        pl.semaphore_signal(
            barrier, inc=1, device_id={"vp": peer // n_cp, "cp": lax.rem(peer, n_cp)},
            device_id_type=pl.DeviceIdType.MESH,
        )
    pl.semaphore_wait(barrier, n - 1 + group - 1)

    waves = (val_hbm, cond_hbm)
    bands = val_hbm.shape[0]
    chip = n_cp * bands
    part = grid // n_cp
    pieces = near_send.shape[-1]
    piece = part // pieces
    side = lax.rem(cp, 2)
    flips = (vp + 1 - 2 * lax.rem(vp, 2), lax.rem(vp + n_vp // 2, n_vp))
    peer_first = (1 - side) * flips[0] + side * flips[1]
    peer_last = (1 - side) * flips[1] + side * flips[0]

    def want_copy(peer, slot):
        return pltpu.make_async_remote_copy(
            src_ref=wanted_ref,
            dst_ref=wanted.at[me],
            send_sem=want_send.at[slot],
            recv_sem=want_recv.at[me],
            device_id={"vp": peer // n_cp, "cp": lax.rem(peer, n_cp)},
            device_id_type=pl.DeviceIdType.MESH,
        )

    def want_arrival(source):
        return pltpu.make_async_remote_copy(
            src_ref=wanted_ref,
            dst_ref=wanted.at[source],
            send_sem=want_send.at[0],
            recv_sem=want_recv.at[source],
            device_id={"vp": vp, "cp": cp},
            device_id_type=pl.DeviceIdType.MESH,
        )

    def near_copy(j, target, owner_cp, a, u, peer):
        return pltpu.make_async_remote_copy(
            src_ref=waves[a].at[:, pl.ds(pl.multiple_of(target * part + u * piece, 128), piece)],
            dst_ref=near.at[a, u, pl.ds(pl.multiple_of(j * chip + owner_cp * bands, bands), bands), :],
            send_sem=near_send.at[j, target, a, u],
            recv_sem=near_recv.at[j, owner_cp, a, u],
            device_id={"vp": peer, "cp": target},
            device_id_type=pl.DeviceIdType.MESH,
        )

    def near_own(a, u):
        return pltpu.make_async_copy(
            waves[a].at[:, pl.ds(pl.multiple_of(cp * part + u * piece, 128), piece)],
            near.at[a, u, pl.ds(pl.multiple_of(cp * bands, bands), bands), :],
            near_recv.at[0, cp, a, u],
        )

    def cross_copy(u):
        return pltpu.make_async_remote_copy(
            src_ref=sent.at[u],
            dst_ref=came.at[u],
            send_sem=cross_send.at[u],
            recv_sem=cross_recv.at[u],
            device_id={"vp": peer_last, "cp": cp},
            device_id_type=pl.DeviceIdType.MESH,
        )

    row_bands = ROW_TILES * TV
    slot_bands = slots * TV
    tile_bands = row_bands + slot_bands

    def give_copies(target, source_cp, u):
        lanes = pl.ds(pl.multiple_of(source_cp * part + u * piece, 128), piece)
        out = []
        for j, (src, dst) in enumerate((
            (pl.ds(0, row_bands), pl.ds(0, row_bands)),
            (
                pl.ds(pl.multiple_of(row_bands + target * slot_bands, 16), slot_bands),
                pl.ds(row_bands, slot_bands),
            ),
        )):
            out.append(pltpu.make_async_remote_copy(
                src_ref=total.at[u, :, src, :],
                dst_ref=ready.at[:, dst, lanes],
                send_sem=give_send.at[target, u, j],
                recv_sem=give_recv.at[source_cp, u, j],
                device_id={"vp": vp, "cp": target},
                device_id_type=pl.DeviceIdType.MESH,
            ))
        return out

    for other in range(1, group):
        want_copy(lax.rem(me + other, group), other - 1).start()
    wanted[me] = wanted_ref[...]

    def launch(u, _):
        for a in range(2):
            for target in range(n_cp):
                near_copy(1, target, cp, a, u, flips[target % 2]).start()
            for target in range(n_cp):
                @pl.when(cp != target)
                def _():
                    near_copy(0, target, cp, a, u, vp).start()
            near_own(a, u).start()
        return 0

    lax.fori_loop(0, pieces, launch, 0)

    def wait_wanted(other, _):
        want_arrival(lax.rem(me + other, group)).wait_recv()
        return 0

    lax.fori_loop(1, group, wait_wanted, 0)

    band = lax.broadcasted_iota(jnp.int32, (2 * chip, wanted.shape[2]), 0)
    band = jnp.where(band < chip, vp * chip + band, peer_first * chip + band - chip)

    def chooser(device, a):
        row = wanted[device][a : a + 1]
        return jnp.where(band == row, 1.0, 0.0).astype(jnp.bfloat16)

    def pick(u, of_chip, put):
        for a in range(2):
            for c in range(n_cp):
                got_rows = lax.dot_general(
                    chooser(of_chip * n_cp + c, a), near[a, u], (((0,), (0,)), ((), ())),
                    preferred_element_type=jnp.float32,
                ).astype(jnp.bfloat16)
                if c == 0:
                    put[u, a, pl.ds(0, row_bands), :] = got_rows[:row_bands]
                put[u, a, pl.ds(row_bands + c * slot_bands, slot_bands), :] = got_rows[row_bands:tile_bands]

    lane = 256 if piece % 256 == 0 else 128

    def densities(start):
        lanes = pl.ds(pl.multiple_of(start, lane), lane)
        val = ready[0, :, lanes].astype(jnp.float32)
        cond = ready[1, :, lanes].astype(jnp.float32)
        row_val = [spread(val[q * TV : (q + 1) * TV]) for q in range(ROW_TILES)]
        row_cond = [spread(cond[q * TC : (q + 1) * TC]) for q in range(ROW_TILES)]
        for q in range(ROW_TILES):
            pair_rows(rho, q * block, row_val[q], twice(cond[q * TC : (q + 1) * TC]), lanes)
        for s in range(slots):
            at = (ROW_TILES + s) * 8
            slot_val, slot_cond = val[at : at + TV], cond[at : at + TC]
            right_val, right_cond = twice(slot_val), twice(slot_cond)
            pair_rows(rho, (ROW_TILES + s) * block, spread(slot_val), right_cond, lanes)
            first = (ROW_TILES + slots + 2 * ROW_TILES * s) * block
            for q in range(ROW_TILES):
                pair_rows(rho, first + q * block, row_val[q], right_val, lanes)
                pair_rows(rho, first + (ROW_TILES + q) * block, row_cond[q], right_cond, lanes)

    def flow(t, _):
        @pl.when(t < pieces)
        def _():
            for a in range(2):
                near_own(a, t).wait()
                for c in range(n_cp):
                    @pl.when(cp != c)
                    def _():
                        near_copy(0, c, c, a, t, vp).wait_recv()
                    near_copy(1, c, c, a, t, vp).wait_recv()
            pick(t, peer_last, sent)
            cross_copy(t).start()
            pick(t, vp, picked)

        u = t - 1

        @pl.when(jnp.logical_and(u >= 0, u < pieces))
        def _():
            cross_copy(u).wait_recv()
            for a in range(2):
                total[u, a] = picked[u, a] + came[u, a]
            for c in range(n_cp):
                @pl.when(cp != c)
                def _():
                    for copy in give_copies(c, cp, u):
                        copy.start()
            lanes = pl.ds(pl.multiple_of(cp * part + u * piece, 128), piece)
            slot_rows = pl.ds(pl.multiple_of(row_bands + cp * slot_bands, 16), slot_bands)
            for a in range(2):
                ready[a, pl.ds(0, row_bands), lanes] = total[u, a, pl.ds(0, row_bands), :]
                ready[a, pl.ds(row_bands, slot_bands), lanes] = total[u, a, slot_rows, :]

        w = t - 2

        @pl.when(w >= 0)
        def _():
            for c in range(n_cp):
                @pl.when(cp != c)
                def _():
                    for copy in give_copies(c, c, w):
                        copy.wait_recv()

            def each(i, _):
                c, j = i // (piece // lane), lax.rem(i, piece // lane)
                densities(c * part + w * piece + j * lane)
                return 0

            lax.fori_loop(0, n_cp * (piece // lane), each, 0)

        return 0

    lax.fori_loop(0, pieces + 2, flow, 0)

    for other in range(1, group):
        want_copy(lax.rem(me + other, group), other - 1).wait_send()

    def landed(u, _):
        for a in range(2):
            for target in range(n_cp):
                near_copy(1, target, cp, a, u, flips[target % 2]).wait_send()

                @pl.when(cp != target)
                def _():
                    near_copy(0, target, cp, a, u, vp).wait_send()
        cross_copy(u).wait_send()
        for target in range(n_cp):
            @pl.when(cp != target)
            def _():
                for copy in give_copies(target, cp, u):
                    copy.wait_send()
        return 0

    lax.fori_loop(0, pieces, landed, 0)

    depth = 1024
    toward = (-1, 1)

    def hop(way, k):
        return pltpu.make_async_remote_copy(
            src_ref=own.at[way, k],
            dst_ref=got.at[way, k],
            send_sem=send_sem.at[way, k],
            recv_sem=recv_sem.at[way, k],
            device_id={"ga": lax.rem(z + toward[way] + n, n)},
            device_id_type=pl.DeviceIdType.MESH,
        )

    far = (n - 1 - z, z)

    def step(i, _):
        @pl.when(i < steps)
        def _():
            first = pl.multiple_of((i // halves) * rows, rows)
            for way in range(2):
                column = pl.multiple_of((way * halves + lax.rem(i, halves)) * width, width)

                for c in range(halves):
                    @pl.when(i == c)
                    def _():
                        copies[way * halves + c].wait()

                acc[...] = jnp.zeros_like(acc)

                def deep(k, _):
                    at = pl.multiple_of(k * depth, depth)
                    acc[...] += jnp.dot(
                        rho[pl.ds(first, rows), pl.ds(at, depth)],
                        basis[pl.ds(at, depth), pl.ds(column, width)],
                        preferred_element_type=jnp.float32,
                    )
                    return 0

                lax.fori_loop(0, grid // depth, deep, 0)
                own[way, i] = acc[...].astype(jnp.bfloat16)

        for way in range(2):
            k = i - LAG * far[way]

            @pl.when(jnp.logical_and(k >= 0, k < steps))
            def _():
                @pl.when(far[way] > 0)
                def _():
                    hop(way, k).wait_recv()
                    summed = own[way, k].astype(jnp.float32) + got[way, k].astype(jnp.float32)
                    own[way, k] = summed.astype(jnp.bfloat16)

                @pl.when(z != ends[way])
                def _():
                    hop(way, k).start()

        return 0

    lax.fori_loop(0, steps + LAG * (n - 1), step, 0)

    share = block // n

    def give(way, k):
        return [
            pltpu.make_async_remote_copy(
                src_ref=mine.at[k],
                dst_ref=there.at[way],
                send_sem=fin_send.at[k, j],
                recv_sem=fin_recv.at[way, j],
                device_id={"ga": k},
                device_id_type=pl.DeviceIdType.MESH,
            )
            for j, (mine, there) in enumerate(((ex_send, ex_got), (dr_send, dr_got)))
        ]

    for way in range(2):
        @pl.when(z == ends[way])
        def _():
            exchange = jnp.zeros(ex_own.shape, jnp.float32)
            for c in range(halves):
                weight = coulomb_ref[:, pl.ds((way * halves + c) * width, width)]
                left = own[way, c, pl.ds(0, ROW_TILES * block), :]
                right = own[way, c, pl.ds(ROW_TILES * block, slots * block), :]
                exchange += weighted_dot(left, weight, right)
            ex_own[...] = exchange
            wide = ROW_TILES * block
            for s in range(slots):
                first = (ROW_TILES + slots + 2 * ROW_TILES * s) * block
                job, at = first // rows, first % rows
                direct = jnp.zeros((wide, wide), jnp.float32)
                for c in range(halves):
                    weight = screen_ref[:, pl.ds((way * halves + c) * width, width)]
                    left = own[way, job * halves + c, pl.ds(at, wide), :]
                    right = own[way, job * halves + c, pl.ds(at + wide, wide), :]
                    direct += weighted_dot(left, weight, right)
                column = lax.broadcasted_iota(jnp.int32, (block, wide), 1)
                dr_own[s] = jnp.where(column < block, direct[:block], direct[block:])
            for k in range(n):
                if k != ends[way]:
                    for q in range(ROW_TILES):
                        ex_send[k, q] = ex_own[pl.ds(q * block + k * share, share), :].astype(jnp.bfloat16)
                    dr_send[k] = dr_own[:, pl.ds(k * share, share), :].astype(jnp.bfloat16)
                    for copy in give(way, k):
                        copy.start()
            for q in range(ROW_TILES):
                exch_ref[q] = ex_own[pl.ds(q * block + ends[way] * share, share), :]
            direct_ref[...] = dr_own[:, pl.ds(ends[way] * share, share), :]

    for way in range(2):
        @pl.when(z != ends[way])
        def _():
            for copy in give(way, 0):
                copy.wait_recv()
            here = ends[1 - way]

            def put(fresh):
                ex_part = ex_got[way].astype(jnp.float32)
                dr_part = dr_got[way].astype(jnp.float32)
                exch_ref[...] = ex_part if fresh else exch_ref[...] + ex_part
                direct_ref[...] = dr_part if fresh else direct_ref[...] + dr_part

            if way == 0:
                pl.when(z == here)(lambda: put(False))
                pl.when(z != here)(lambda: put(True))
            else:
                put(False)

    for way in range(2):
        @pl.when(z != ends[way])
        def _():
            def drain(k, _):
                hop(way, k).wait_send()
                return 0

            lax.fori_loop(0, steps, drain, 0)

        @pl.when(z == ends[way])
        def _():
            for k in range(n):
                if k != ends[way]:
                    for copy in give(way, k):
                        copy.wait_send()


def make_tiles(sizes, slots, val, cond, wanted, basis, screen, coulomb):
    n, n_vp, n_cp = sizes
    grid, rank = basis.shape
    bands = val.shape[0]
    width = rank // 4
    block = TV * TC
    rows = (ROW_TILES + slots) * block
    total = (ROW_TILES + slots + 2 * ROW_TILES * slots) * block
    steps = (total // rows) * 2
    share = block // n
    part = grid // n_cp
    pieces = max(u for u in range(1, 5) if part % (u * 128) == 0)
    piece = part // pieces
    picked = (ROW_TILES + n_cp * slots) * TV
    vmem = pl.BlockSpec(memory_space=pltpu.VMEM)
    anywhere = pl.BlockSpec(memory_space=pl.ANY)
    bf16, f32 = jnp.bfloat16, jnp.float32
    return pl.pallas_call(
        functools.partial(tiles_kernel, n, n_vp, n_cp, slots),
        out_shape=(
            jax.ShapeDtypeStruct((ROW_TILES, share, slots * block), f32),
            jax.ShapeDtypeStruct((slots, share, ROW_TILES * block), f32),
        ),
        in_specs=[anywhere, anywhere, vmem, anywhere, vmem, vmem],
        out_specs=(vmem, vmem),
        scratch_shapes=[
            pltpu.VMEM((n_vp * n_cp,) + wanted.shape, jnp.int32),
            pltpu.VMEM((2, pieces, 2 * n_cp * bands, piece), bf16),
            pltpu.VMEM((pieces, 2, picked, piece), bf16),
            pltpu.VMEM((pieces, 2, picked, piece), bf16),
            pltpu.VMEM((pieces, 2, picked, piece), bf16),
            pltpu.VMEM((pieces, 2, picked, piece), bf16),
            pltpu.VMEM((2, (ROW_TILES + slots) * TV, grid), bf16),
            pltpu.VMEM((grid, rank), bf16),
            pltpu.VMEM((total, grid), bf16),
            pltpu.VMEM((rows, width), f32),
            pltpu.VMEM((2, steps, rows, width), bf16),
            pltpu.VMEM((2, steps, rows, width), bf16),
            pltpu.VMEM((ROW_TILES * block, slots * block), f32),
            pltpu.VMEM((slots, block, ROW_TILES * block), f32),
            pltpu.VMEM((n, ROW_TILES, share, slots * block), bf16),
            pltpu.VMEM((n, slots, share, ROW_TILES * block), bf16),
            pltpu.VMEM((2, ROW_TILES, share, slots * block), bf16),
            pltpu.VMEM((2, slots, share, ROW_TILES * block), bf16),
            pltpu.SemaphoreType.DMA((n_vp * n_cp,)),
            pltpu.SemaphoreType.DMA((n_vp * n_cp,)),
            pltpu.SemaphoreType.DMA((2, n_cp, 2, pieces)),
            pltpu.SemaphoreType.DMA((2, n_cp, 2, pieces)),
            pltpu.SemaphoreType.DMA((pieces,)),
            pltpu.SemaphoreType.DMA((pieces,)),
            pltpu.SemaphoreType.DMA((n_cp, pieces, 2)),
            pltpu.SemaphoreType.DMA((n_cp, pieces, 2)),
            pltpu.SemaphoreType.DMA((4,)),
            pltpu.SemaphoreType.DMA((2, steps)),
            pltpu.SemaphoreType.DMA((2, steps)),
            pltpu.SemaphoreType.DMA((n, 2)),
            pltpu.SemaphoreType.DMA((2, 2)),
        ],
        compiler_params=pltpu.CompilerParams(
            collective_id=0, has_side_effects=True, vmem_limit_bytes=67043328
        ),
    )(val, cond, wanted, basis, screen, coulomb)


def shards(valence_wavefunction, cond_wave, screen_basis, screen, coulomb, window_rows, tile_owner):
    slots = tile_owner.shape[0]
    n = lax.axis_size("ga")
    sizes = (n, lax.axis_size("vp"), lax.axis_size("cp"))
    pair_tiles = jnp.concatenate([window_rows, tile_owner])
    each = jnp.arange(TV, dtype=jnp.int32)[None, :]
    wanted = jnp.stack(
        [
            ((pair_tiles // NCT)[:, None] * TV + each).reshape(-1),
            ((pair_tiles % NCT)[:, None] * TC + each).reshape(-1),
        ]
    )
    wanted = jnp.pad(wanted, ((0, 6), (0, 128 - wanted.shape[1])), constant_values=-1)
    exchange, direct = make_tiles(
        sizes, slots, valence_wavefunction, cond_wave, wanted, screen_basis, screen[None], coulomb[None]
    )
    v = TV // n
    exchange = exchange.reshape(2, v, TC, slots, TV, TC).transpose(0, 3, 1, 2, 4, 5)
    direct = direct.reshape(slots, v, TV, 2, TC, TC).transpose(3, 0, 1, 4, 2, 5)
    kernel = (2.0 * exchange - direct).reshape(2, slots, -1)
    live = (tile_owner[None, :] >= window_rows[:, None])[:, :, None]
    return jnp.where(live, kernel, jnp.zeros_like(kernel))


def solution(mesh):
    in_specs = (
        P(("vp", "cp"), "ga"),
        P(("vp", "cp"), "ga"),
        P("ga", None),
        P(),
        P(),
        P(),
        P(("vp", "cp")),
    )
    out_specs = P(None, ("vp", "cp"), "ga")
    return jax.shard_map(shards, mesh=mesh, in_specs=in_specs, out_specs=out_specs, check_vma=False)
```

```python
import functools
import jax
import jax.numpy as jnp
from jax import lax
from jax.experimental import pallas as pl
from jax.experimental.pallas import tpu as pltpu
from jax.sharding import PartitionSpec as P

TV = 8
TC = 8
NCT = 64
LAG = 2
ROW_TILES = 2
PAIR = 2
QUARTERS = 4


def pair_rows(rho, first, left, right, lanes):
    for i in range(len(left)):
        rho[pl.ds(first + 16 * i, 16), lanes] = left[i] * right


def spread(tile):
    out = []
    for i in range(0, tile.shape[0], 2):
        two = [jnp.broadcast_to(tile[i + j : i + j + 1], (8, tile.shape[1])) for j in range(2)]
        out.append(jnp.concatenate(two, axis=0).astype(jnp.bfloat16))
    return out


def twice(tile):
    return jnp.concatenate([tile, tile], axis=0).astype(jnp.bfloat16)


def dot_t(a, b):
    return lax.dot_general(a, b, (((1,), (1,)), ((), ())), preferred_element_type=jnp.float32)


def weighted_dot(a, weight, b):
    scaled = a.astype(jnp.float32) * weight
    high = scaled.astype(jnp.bfloat16)
    low = (scaled - high.astype(jnp.float32)).astype(jnp.bfloat16)
    return dot_t(high, b) + dot_t(low, b)


def tiles_kernel(
    n, n_vp, n_cp, slots, val_hbm, cond_hbm, wanted_ref, basis_hbm, screen_ref, coulomb_ref,
    exch_ref, direct_ref, wanted, near, picked, sent, came, total, ready, basis, rho, acc, own, got, ex_own, dr_own, ex_send, dr_send, ex_got, dr_got,
    want_send, want_recv, near_send, near_recv, cross_send, cross_recv, give_send, give_recv,
    basis_sem, send_sem, recv_sem, fin_send, fin_recv,
):
    z = lax.axis_index("ga")
    grid, rank = basis_hbm.shape
    steps, quarters, quarter, width = own.shape[1:]
    rows = quarters * quarter
    halves = rank // (2 * width)
    ends = (0, n - 1)
    block = TV * TC

    copies = []
    for c in range(2 * halves):
        cols = pl.ds(c * width, width)
        copy = pltpu.make_async_copy(basis_hbm.at[:, cols], basis.at[:, cols], basis_sem.at[c])
        copy.start()
        copies.append(copy)

    barrier = pltpu.get_barrier_semaphore()
    for other in range(1, n):
        pl.semaphore_signal(
            barrier, inc=1, device_id={"ga": lax.rem(z + other, n)}, device_id_type=pl.DeviceIdType.MESH
        )

    vp, cp = lax.axis_index("vp"), lax.axis_index("cp")
    group = n_vp * n_cp
    me = vp * n_cp + cp
    for other in range(1, group):
        peer = lax.rem(me + other, group)
        pl.semaphore_signal(
            barrier, inc=1, device_id={"vp": peer // n_cp, "cp": lax.rem(peer, n_cp)},
            device_id_type=pl.DeviceIdType.MESH,
        )
    pl.semaphore_wait(barrier, n - 1 + group - 1)

    waves = (val_hbm, cond_hbm)
    bands = val_hbm.shape[0]
    chip = n_cp * bands
    part = grid // n_cp
    pieces = near_send.shape[-1]
    piece = part // pieces
    side = lax.rem(cp, 2)
    flips = (vp + 1 - 2 * lax.rem(vp, 2), lax.rem(vp + n_vp // 2, n_vp))
    peer_first = (1 - side) * flips[0] + side * flips[1]
    peer_last = (1 - side) * flips[1] + side * flips[0]

    def want_copy(peer, slot):
        return pltpu.make_async_remote_copy(
            src_ref=wanted_ref,
            dst_ref=wanted.at[me],
            send_sem=want_send.at[slot],
            recv_sem=want_recv.at[me],
            device_id={"vp": peer // n_cp, "cp": lax.rem(peer, n_cp)},
            device_id_type=pl.DeviceIdType.MESH,
        )

    def want_arrival(source):
        return pltpu.make_async_remote_copy(
            src_ref=wanted_ref,
            dst_ref=wanted.at[source],
            send_sem=want_send.at[0],
            recv_sem=want_recv.at[source],
            device_id={"vp": vp, "cp": cp},
            device_id_type=pl.DeviceIdType.MESH,
        )

    def near_copy(j, target, owner_cp, a, u, peer):
        return pltpu.make_async_remote_copy(
            src_ref=waves[a].at[:, pl.ds(pl.multiple_of(target * part + u * piece, 128), piece)],
            dst_ref=near.at[a, u, pl.ds(pl.multiple_of(j * chip + owner_cp * bands, bands), bands), :],
            send_sem=near_send.at[j, target, a, u],
            recv_sem=near_recv.at[j, owner_cp, a, u],
            device_id={"vp": peer, "cp": target},
            device_id_type=pl.DeviceIdType.MESH,
        )

    def near_own(a, u):
        return pltpu.make_async_copy(
            waves[a].at[:, pl.ds(pl.multiple_of(cp * part + u * piece, 128), piece)],
            near.at[a, u, pl.ds(pl.multiple_of(cp * bands, bands), bands), :],
            near_recv.at[0, cp, a, u],
        )

    row_bands = ROW_TILES * TV
    pair_bands = PAIR * TV
    groups = slots // PAIR

    def cross_copies(u, p):
        spans = [pl.ds(pl.multiple_of(row_bands + p * n_cp * pair_bands, 16), n_cp * pair_bands)]
        if isinstance(p, int) and p == 0:
            spans = [pl.ds(0, row_bands + n_cp * pair_bands)]
        return [
            pltpu.make_async_remote_copy(
                src_ref=sent.at[u, :, span, :],
                dst_ref=came.at[u, :, span, :],
                send_sem=cross_send.at[u, p],
                recv_sem=cross_recv.at[u, p],
                device_id={"vp": peer_last, "cp": cp},
                device_id_type=pl.DeviceIdType.MESH,
            )
            for span in spans
        ]

    def give_copies(target, source_cp, u, p):
        lanes = pl.ds(pl.multiple_of(source_cp * part + u * piece, 128), piece)
        spans = [
            (
                pl.ds(pl.multiple_of(row_bands + (p * n_cp + target) * pair_bands, 16), pair_bands),
                pl.ds(pl.multiple_of(row_bands + p * pair_bands, 16), pair_bands),
                p,
            )
        ]
        if isinstance(p, int) and p == 0:
            spans.append((pl.ds(0, row_bands), pl.ds(0, row_bands), groups))
        return [
            pltpu.make_async_remote_copy(
                src_ref=total.at[u, :, src, :],
                dst_ref=ready.at[:, dst, lanes],
                send_sem=give_send.at[target, u, j],
                recv_sem=give_recv.at[source_cp, u, j],
                device_id={"vp": vp, "cp": target},
                device_id_type=pl.DeviceIdType.MESH,
            )
            for src, dst, j in spans
        ]

    for other in range(1, group):
        want_copy(lax.rem(me + other, group), other - 1).start()
    wanted[me] = wanted_ref[...]

    def launch(u, _):
        for a in range(2):
            for target in range(n_cp):
                near_copy(1, target, cp, a, u, flips[target % 2]).start()
            for target in range(n_cp):
                @pl.when(cp != target)
                def _():
                    near_copy(0, target, cp, a, u, vp).start()
            near_own(a, u).start()
        return 0

    lax.fori_loop(0, pieces, launch, 0)

    def wait_wanted(other, _):
        want_arrival(lax.rem(me + other, group)).wait_recv()
        return 0

    lax.fori_loop(1, group, wait_wanted, 0)

    band = lax.broadcasted_iota(jnp.int32, (2 * chip, wanted.shape[2]), 0)
    band = jnp.where(band < chip, vp * chip + band, peer_first * chip + band - chip)

    def chooser(device, a):
        row = wanted[device][a : a + 1]
        return jnp.where(band == row, 1.0, 0.0).astype(jnp.bfloat16)

    def pick(u, of_chip, put):
        for a in range(2):
            for c in range(n_cp):
                got_rows = lax.dot_general(
                    chooser(of_chip * n_cp + c, a), near[a, u], (((0,), (0,)), ((), ())),
                    preferred_element_type=jnp.float32,
                ).astype(jnp.bfloat16)
                if c == 0:
                    put[u, a, pl.ds(0, row_bands), :] = got_rows[:row_bands]
                for p in range(groups):
                    put[u, a, pl.ds(row_bands + (p * n_cp + c) * pair_bands, pair_bands), :] = got_rows[
                        row_bands + p * pair_bands : row_bands + (p + 1) * pair_bands
                    ]

    lane = 256 if piece % 256 == 0 else 128

    def densities(start, p, with_rows):
        lanes = pl.ds(pl.multiple_of(start, lane), lane)
        val = ready[0, pl.ds(0, row_bands), lanes].astype(jnp.float32)
        cond = ready[1, pl.ds(0, row_bands), lanes].astype(jnp.float32)
        row_val = [spread(val[q * TV : (q + 1) * TV]) for q in range(ROW_TILES)]
        row_cond = [spread(cond[q * TC : (q + 1) * TC]) for q in range(ROW_TILES)]
        last = groups * rows
        if with_rows:
            for q in range(ROW_TILES):
                pair_rows(rho, last + q * block, row_val[q], twice(cond[q * TC : (q + 1) * TC]), lanes)
        span = pl.ds(pl.multiple_of(row_bands + p * pair_bands, 16), pair_bands)
        val = ready[0, span, lanes].astype(jnp.float32)
        cond = ready[1, span, lanes].astype(jnp.float32)
        for s in range(PAIR):
            slot_val, slot_cond = val[s * TV : (s + 1) * TV], cond[s * TC : (s + 1) * TC]
            right_val, right_cond = twice(slot_val), twice(slot_cond)
            at = pl.multiple_of(last + (ROW_TILES + p * PAIR + s) * block, block)
            pair_rows(rho, at, spread(slot_val), right_cond, lanes)
            first = pl.multiple_of(p * rows + 2 * ROW_TILES * s * block, block)
            for q in range(ROW_TILES):
                pair_rows(rho, first + q * block, row_val[q], right_val, lanes)
                pair_rows(rho, first + (ROW_TILES + q) * block, row_cond[q], right_cond, lanes)

    def hand_out(u, p):
        lanes = pl.ds(pl.multiple_of(cp * part + u * piece, 128), piece)
        for copy in cross_copies(u, p):
            copy.wait_recv()
        span = pl.ds(pl.multiple_of(row_bands + p * n_cp * pair_bands, 16), n_cp * pair_bands)
        mine = pl.ds(pl.multiple_of(row_bands + (p * n_cp + cp) * pair_bands, 16), pair_bands)
        home = pl.ds(pl.multiple_of(row_bands + p * pair_bands, 16), pair_bands)
        spans = [(span, mine, home)]
        if isinstance(p, int) and p == 0:
            tiles = pl.ds(0, row_bands)
            spans.append((tiles, tiles, tiles))
        for a in range(2):
            for span, mine, home in spans:
                total[u, a, span, :] = picked[u, a, span, :] + came[u, a, span, :]
                ready[a, home, lanes] = total[u, a, mine, :]
        for c in range(n_cp):
            @pl.when(cp != c)
            def _():
                for copy in give_copies(c, cp, u, p):
                    copy.start()

    def take_in(u, p):
        for c in range(n_cp):
            @pl.when(cp != c)
            def _():
                for copy in give_copies(c, c, u, p):
                    copy.wait_recv()

        def each(i, _):
            c, j = i // (piece // lane), lax.rem(i, piece // lane)
            densities(c * part + u * piece + j * lane, p, isinstance(p, int) and p == 0)
            return 0

        lax.fori_loop(0, n_cp * (piece // lane), each, 0)

    def flow(t, _):
        @pl.when(t < pieces)
        def _():
            for a in range(2):
                near_own(a, t).wait()
                for c in range(n_cp):
                    @pl.when(cp != c)
                    def _():
                        near_copy(0, c, c, a, t, vp).wait_recv()
                    near_copy(1, c, c, a, t, vp).wait_recv()
            pick(t, peer_last, sent)
            for copy in cross_copies(t, 0):
                copy.start()
            pick(t, vp, picked)

            @pl.when(t == pieces - 1)
            def _():
                def later(i, _):
                    for copy in cross_copies(lax.rem(i, pieces), 1 + i // pieces):
                        copy.start()
                    return 0

                lax.fori_loop(0, pieces * (groups - 1), later, 0)

        @pl.when(jnp.logical_and(t >= 1, t <= pieces))
        def _():
            hand_out(t - 1, 0)

        @pl.when(t >= 2)
        def _():
            take_in(t - 2, 0)

        return 0

    lax.fori_loop(0, pieces + 2, flow, 0)

    depth = 1024
    toward = (-1, 1)

    def hop(way, k, h):
        return pltpu.make_async_remote_copy(
            src_ref=own.at[way, k, h],
            dst_ref=got.at[way, k, h],
            send_sem=send_sem.at[way, k, h],
            recv_sem=recv_sem.at[way, k, h],
            device_id={"ga": lax.rem(z + toward[way] + n, n)},
            device_id_type=pl.DeviceIdType.MESH,
        )

    far = (n - 1 - z, z)

    def step(i, _):
        @pl.when(i < steps)
        def _():
            first = pl.multiple_of((i // halves) * rows, rows)
            for way in range(2):
                column = pl.multiple_of((way * halves + lax.rem(i, halves)) * width, width)

                for c in range(halves):
                    @pl.when(i == c)
                    def _():
                        copies[way * halves + c].wait()

                acc[...] = jnp.zeros_like(acc)

                def deep(k, _):
                    at = pl.multiple_of(k * depth, depth)
                    acc[...] += jnp.dot(
                        rho[pl.ds(first, rows), pl.ds(at, depth)],
                        basis[pl.ds(at, depth), pl.ds(column, width)],
                        preferred_element_type=jnp.float32,
                    )
                    return 0

                lax.fori_loop(0, grid // depth, deep, 0)
                for h in range(QUARTERS):
                    own[way, i, h] = acc[pl.ds(h * (rows // QUARTERS), rows // QUARTERS), :].astype(jnp.bfloat16)

        for h in range(QUARTERS):
            for way in range(2):
                k = i - LAG * far[way]

                @pl.when(jnp.logical_and(k >= 0, k < steps))
                def _():
                    @pl.when(far[way] > 0)
                    def _():
                        hop(way, k, h).wait_recv()
                        summed = own[way, k, h].astype(jnp.float32) + got[way, k, h].astype(jnp.float32)
                        own[way, k, h] = summed.astype(jnp.bfloat16)

                    @pl.when(z != ends[way])
                    def _():
                        hop(way, k, h).start()

        after = 1 + i // halves

        @pl.when(jnp.logical_and(after < groups, lax.rem(i, halves) == 0))
        def _():
            def out(u, _):
                hand_out(u, after)
                return 0

            lax.fori_loop(0, pieces, out, 0)

        @pl.when(jnp.logical_and(after < groups, lax.rem(i, halves) == halves - 1))
        def _():
            def into(u, _):
                take_in(u, after)
                return 0

            lax.fori_loop(0, pieces, into, 0)

        return 0

    lax.fori_loop(0, steps + LAG * (n - 1), step, 0)

    share = block // n

    def give(way, k):
        return [
            pltpu.make_async_remote_copy(
                src_ref=mine.at[k],
                dst_ref=there.at[way],
                send_sem=fin_send.at[k, j],
                recv_sem=fin_recv.at[way, j],
                device_id={"ga": k},
                device_id_type=pl.DeviceIdType.MESH,
            )
            for j, (mine, there) in enumerate(((ex_send, ex_got), (dr_send, dr_got)))
        ]

    for way in range(2):
        @pl.when(z == ends[way])
        def _():
            exchange = jnp.zeros(ex_own.shape, jnp.float32)
            for c in range(halves):
                weight = coulomb_ref[:, pl.ds((way * halves + c) * width, width)]
                whole = own[way, groups * halves + c].reshape(rows, width)
                left, right = whole[: ROW_TILES * block], whole[ROW_TILES * block :]
                exchange += weighted_dot(left, weight, right)
            ex_own[...] = exchange
            wide = ROW_TILES * block
            for s in range(slots):
                job, at = s // PAIR, (s % PAIR) * 2 * wide
                direct = jnp.zeros((wide, wide), jnp.float32)
                for c in range(halves):
                    weight = screen_ref[:, pl.ds((way * halves + c) * width, width)]
                    whole = own[way, job * halves + c].reshape(rows, width)
                    left, right = whole[at : at + wide], whole[at + wide : at + 2 * wide]
                    direct += weighted_dot(left, weight, right)
                column = lax.broadcasted_iota(jnp.int32, (block, wide), 1)
                dr_own[s] = jnp.where(column < block, direct[:block], direct[block:])
            for k in range(n):
                if k != ends[way]:
                    for q in range(ROW_TILES):
                        ex_send[k, q] = ex_own[pl.ds(q * block + k * share, share), :].astype(jnp.bfloat16)
                    dr_send[k] = dr_own[:, pl.ds(k * share, share), :].astype(jnp.bfloat16)
                    for copy in give(way, k):
                        copy.start()
            for q in range(ROW_TILES):
                exch_ref[q] = ex_own[pl.ds(q * block + ends[way] * share, share), :]
            direct_ref[...] = dr_own[:, pl.ds(ends[way] * share, share), :]

    for way in range(2):
        @pl.when(z != ends[way])
        def _():
            for copy in give(way, 0):
                copy.wait_recv()
            here = ends[1 - way]

            def put(fresh):
                ex_part = ex_got[way].astype(jnp.float32)
                dr_part = dr_got[way].astype(jnp.float32)
                exch_ref[...] = ex_part if fresh else exch_ref[...] + ex_part
                direct_ref[...] = dr_part if fresh else direct_ref[...] + dr_part

            if way == 0:
                pl.when(z == here)(lambda: put(False))
                pl.when(z != here)(lambda: put(True))
            else:
                put(False)

    for way in range(2):
        @pl.when(z != ends[way])
        def _():
            def drain(k, _):
                for h in range(QUARTERS):
                    hop(way, k, h).wait_send()
                return 0

            lax.fori_loop(0, steps, drain, 0)

        @pl.when(z == ends[way])
        def _():
            for k in range(n):
                if k != ends[way]:
                    for copy in give(way, k):
                        copy.wait_send()

    for other in range(1, group):
        want_copy(lax.rem(me + other, group), other - 1).wait_send()

    def landed(u, _):
        for a in range(2):
            for target in range(n_cp):
                near_copy(1, target, cp, a, u, flips[target % 2]).wait_send()

                @pl.when(cp != target)
                def _():
                    near_copy(0, target, cp, a, u, vp).wait_send()
        for p in range(groups):
            for copy in cross_copies(u, p):
                copy.wait_send()
            for target in range(n_cp):
                @pl.when(cp != target)
                def _():
                    for copy in give_copies(target, cp, u, p):
                        copy.wait_send()
        return 0

    lax.fori_loop(0, pieces, landed, 0)


def make_tiles(sizes, slots, val, cond, wanted, basis, screen, coulomb):
    n, n_vp, n_cp = sizes
    grid, rank = basis.shape
    bands = val.shape[0]
    width = rank // 4
    block = TV * TC
    rows = (ROW_TILES + slots) * block
    total = (ROW_TILES + slots + 2 * ROW_TILES * slots) * block
    steps = (total // rows) * 2
    share = block // n
    part = grid // n_cp
    pieces = max(u for u in range(1, 5) if part % (u * 128) == 0)
    piece = part // pieces
    picked = (ROW_TILES + n_cp * slots) * TV
    vmem = pl.BlockSpec(memory_space=pltpu.VMEM)
    anywhere = pl.BlockSpec(memory_space=pl.ANY)
    bf16, f32 = jnp.bfloat16, jnp.float32
    return pl.pallas_call(
        functools.partial(tiles_kernel, n, n_vp, n_cp, slots),
        out_shape=(
            jax.ShapeDtypeStruct((ROW_TILES, share, slots * block), f32),
            jax.ShapeDtypeStruct((slots, share, ROW_TILES * block), f32),
        ),
        in_specs=[anywhere, anywhere, vmem, anywhere, vmem, vmem],
        out_specs=(vmem, vmem),
        scratch_shapes=[
            pltpu.VMEM((n_vp * n_cp,) + wanted.shape, jnp.int32),
            pltpu.VMEM((2, pieces, 2 * n_cp * bands, piece), bf16),
            pltpu.VMEM((pieces, 2, picked, piece), bf16),
            pltpu.VMEM((pieces, 2, picked, piece), bf16),
            pltpu.VMEM((pieces, 2, picked, piece), bf16),
            pltpu.VMEM((pieces, 2, picked, piece), bf16),
            pltpu.VMEM((2, (ROW_TILES + slots) * TV, grid), bf16),
            pltpu.VMEM((grid, rank), bf16),
            pltpu.VMEM((total, grid), bf16),
            pltpu.VMEM((rows, width), f32),
            pltpu.VMEM((2, steps, QUARTERS, rows // QUARTERS, width), bf16),
            pltpu.VMEM((2, steps, QUARTERS, rows // QUARTERS, width), bf16),
            pltpu.VMEM((ROW_TILES * block, slots * block), f32),
            pltpu.VMEM((slots, block, ROW_TILES * block), f32),
            pltpu.VMEM((n, ROW_TILES, share, slots * block), bf16),
            pltpu.VMEM((n, slots, share, ROW_TILES * block), bf16),
            pltpu.VMEM((2, ROW_TILES, share, slots * block), bf16),
            pltpu.VMEM((2, slots, share, ROW_TILES * block), bf16),
            pltpu.SemaphoreType.DMA((n_vp * n_cp,)),
            pltpu.SemaphoreType.DMA((n_vp * n_cp,)),
            pltpu.SemaphoreType.DMA((2, n_cp, 2, pieces)),
            pltpu.SemaphoreType.DMA((2, n_cp, 2, pieces)),
            pltpu.SemaphoreType.DMA((pieces, slots // PAIR)),
            pltpu.SemaphoreType.DMA((pieces, slots // PAIR)),
            pltpu.SemaphoreType.DMA((n_cp, pieces, slots // PAIR + 1)),
            pltpu.SemaphoreType.DMA((n_cp, pieces, slots // PAIR + 1)),
            pltpu.SemaphoreType.DMA((4,)),
            pltpu.SemaphoreType.DMA((2, steps, QUARTERS)),
            pltpu.SemaphoreType.DMA((2, steps, QUARTERS)),
            pltpu.SemaphoreType.DMA((n, 2)),
            pltpu.SemaphoreType.DMA((2, 2)),
        ],
        compiler_params=pltpu.CompilerParams(
            collective_id=0, has_side_effects=True, vmem_limit_bytes=67043328
        ),
    )(val, cond, wanted, basis, screen, coulomb)


def shards(valence_wavefunction, cond_wave, screen_basis, screen, coulomb, window_rows, tile_owner):
    slots = tile_owner.shape[0]
    n = lax.axis_size("ga")
    sizes = (n, lax.axis_size("vp"), lax.axis_size("cp"))
    pair_tiles = jnp.concatenate([window_rows, tile_owner])
    each = jnp.arange(TV, dtype=jnp.int32)[None, :]
    wanted = jnp.stack(
        [
            ((pair_tiles // NCT)[:, None] * TV + each).reshape(-1),
            ((pair_tiles % NCT)[:, None] * TC + each).reshape(-1),
        ]
    )
    wanted = jnp.pad(wanted, ((0, 6), (0, 128 - wanted.shape[1])), constant_values=-1)
    exchange, direct = make_tiles(
        sizes, slots, valence_wavefunction, cond_wave, wanted, screen_basis, screen[None], coulomb[None]
    )
    v = TV // n
    exchange = exchange.reshape(2, v, TC, slots, TV, TC).transpose(0, 3, 1, 2, 4, 5)
    direct = direct.reshape(slots, v, TV, 2, TC, TC).transpose(3, 0, 1, 4, 2, 5)
    kernel = (2.0 * exchange - direct).reshape(2, slots, -1)
    live = (tile_owner[None, :] >= window_rows[:, None])[:, :, None]
    return jnp.where(live, kernel, jnp.zeros_like(kernel))


def solution(mesh):
    in_specs = (
        P(("vp", "cp"), "ga"),
        P(("vp", "cp"), "ga"),
        P("ga", None),
        P(),
        P(),
        P(),
        P(("vp", "cp")),
    )
    out_specs = P(None, ("vp", "cp"), "ga")
    return jax.shard_map(shards, mesh=mesh, in_specs=in_specs, out_specs=out_specs, check_vma=False)
```

```python
import functools
import jax
import jax.numpy as jnp
from jax import lax
from jax.experimental import pallas as pl
from jax.experimental.pallas import tpu as pltpu
from jax.sharding import PartitionSpec as P

TV = 8
TC = 8
NCT = 64
LAG = 1
ROW_TILES = 2
PAIR = 2
QUARTERS = 4


def pair_rows(rho, first, left, right, lanes):
    for i in range(len(left)):
        rho[pl.ds(first + 16 * i, 16), lanes] = left[i] * right


def spread(tile):
    out = []
    for i in range(0, tile.shape[0], 2):
        two = [jnp.broadcast_to(tile[i + j : i + j + 1], (8, tile.shape[1])) for j in range(2)]
        out.append(jnp.concatenate(two, axis=0).astype(jnp.bfloat16))
    return out


def twice(tile):
    return jnp.concatenate([tile, tile], axis=0).astype(jnp.bfloat16)


def dot_t(a, b):
    return lax.dot_general(a, b, (((1,), (1,)), ((), ())), preferred_element_type=jnp.float32)


def weighted_dot(a, weight, b):
    scaled = a.astype(jnp.float32) * weight
    high = scaled.astype(jnp.bfloat16)
    low = (scaled - high.astype(jnp.float32)).astype(jnp.bfloat16)
    return dot_t(high, b) + dot_t(low, b)


def tiles_kernel(
    n, n_vp, n_cp, slots, val_hbm, cond_hbm, wanted_ref, basis_hbm, screen_ref, coulomb_ref,
    exch_ref, direct_ref, wanted, chosen, near, picked, sent, came, total, ready, basis, rho, acc, own, got, ex_own, dr_own, ex_send, dr_send, ex_got, dr_got,
    want_send, want_recv, near_send, near_recv, cross_send, cross_recv, give_send, give_recv,
    basis_sem, send_sem, recv_sem, fin_send, fin_recv,
):
    z = lax.axis_index("ga")
    grid, rank = basis_hbm.shape
    steps, quarters, quarter, width = own.shape[1:]
    rows = quarters * quarter
    halves = rank // (2 * width)
    ends = (0, n - 1)
    block = TV * TC

    copies = []
    for c in range(2 * halves):
        cols = pl.ds(c * width, width)
        copy = pltpu.make_async_copy(basis_hbm.at[:, cols], basis.at[:, cols], basis_sem.at[c])
        copy.start()
        copies.append(copy)

    barrier = pltpu.get_barrier_semaphore()
    for other in range(1, n):
        pl.semaphore_signal(
            barrier, inc=1, device_id={"ga": lax.rem(z + other, n)}, device_id_type=pl.DeviceIdType.MESH
        )

    vp, cp = lax.axis_index("vp"), lax.axis_index("cp")
    group = n_vp * n_cp
    me = vp * n_cp + cp
    for other in range(1, group):
        peer = lax.rem(me + other, group)
        pl.semaphore_signal(
            barrier, inc=1, device_id={"vp": peer // n_cp, "cp": lax.rem(peer, n_cp)},
            device_id_type=pl.DeviceIdType.MESH,
        )
    pl.semaphore_wait(barrier, n - 1 + group - 1)

    waves = (val_hbm, cond_hbm)
    bands = val_hbm.shape[0]
    chip = n_cp * bands
    part = grid // n_cp
    pieces = near_send.shape[-1]
    piece = part // pieces
    side = lax.rem(cp, 2)
    flips = (vp + 1 - 2 * lax.rem(vp, 2), lax.rem(vp + n_vp // 2, n_vp))
    peer_first = (1 - side) * flips[0] + side * flips[1]
    peer_last = (1 - side) * flips[1] + side * flips[0]

    def want_copy(peer, slot):
        return pltpu.make_async_remote_copy(
            src_ref=wanted_ref,
            dst_ref=wanted.at[me],
            send_sem=want_send.at[slot],
            recv_sem=want_recv.at[me],
            device_id={"vp": peer // n_cp, "cp": lax.rem(peer, n_cp)},
            device_id_type=pl.DeviceIdType.MESH,
        )

    def want_arrival(source):
        return pltpu.make_async_remote_copy(
            src_ref=wanted_ref,
            dst_ref=wanted.at[source],
            send_sem=want_send.at[0],
            recv_sem=want_recv.at[source],
            device_id={"vp": vp, "cp": cp},
            device_id_type=pl.DeviceIdType.MESH,
        )

    def near_copy(j, target, owner_cp, a, u, peer):
        return pltpu.make_async_remote_copy(
            src_ref=waves[a].at[:, pl.ds(pl.multiple_of(target * part + u * piece, 128), piece)],
            dst_ref=near.at[a, u, pl.ds(pl.multiple_of(j * chip + owner_cp * bands, bands), bands), :],
            send_sem=near_send.at[j, target, a, u],
            recv_sem=near_recv.at[j, owner_cp, a, u],
            device_id={"vp": peer, "cp": target},
            device_id_type=pl.DeviceIdType.MESH,
        )

    def near_own(a, u):
        return pltpu.make_async_copy(
            waves[a].at[:, pl.ds(pl.multiple_of(cp * part + u * piece, 128), piece)],
            near.at[a, u, pl.ds(pl.multiple_of(cp * bands, bands), bands), :],
            near_recv.at[0, cp, a, u],
        )

    row_bands = ROW_TILES * TV
    pair_bands = PAIR * TV
    groups = slots // PAIR

    def cross_copies(u, p):
        spans = [pl.ds(pl.multiple_of(row_bands + p * n_cp * pair_bands, 16), n_cp * pair_bands)]
        if isinstance(p, int) and p == 0:
            spans = [pl.ds(0, row_bands + n_cp * pair_bands)]
        return [
            pltpu.make_async_remote_copy(
                src_ref=sent.at[u, :, span, :],
                dst_ref=came.at[u, :, span, :],
                send_sem=cross_send.at[u, p],
                recv_sem=cross_recv.at[u, p],
                device_id={"vp": peer_last, "cp": cp},
                device_id_type=pl.DeviceIdType.MESH,
            )
            for span in spans
        ]

    def give_copies(target, source_cp, u, p):
        lanes = pl.ds(pl.multiple_of(source_cp * part + u * piece, 128), piece)
        spans = [
            (
                pl.ds(pl.multiple_of(row_bands + (p * n_cp + target) * pair_bands, 16), pair_bands),
                pl.ds(pl.multiple_of(row_bands + p * pair_bands, 16), pair_bands),
                p,
            )
        ]
        if isinstance(p, int) and p == 0:
            spans.append((pl.ds(0, row_bands), pl.ds(0, row_bands), groups))
        return [
            pltpu.make_async_remote_copy(
                src_ref=total.at[u, :, src, :],
                dst_ref=ready.at[:, dst, lanes],
                send_sem=give_send.at[target, u, j],
                recv_sem=give_recv.at[source_cp, u, j],
                device_id={"vp": vp, "cp": target},
                device_id_type=pl.DeviceIdType.MESH,
            )
            for src, dst, j in spans
        ]

    for other in range(1, group):
        want_copy(lax.rem(me + other, group), other - 1).start()
    wanted[me] = wanted_ref[...]

    def launch(u, _):
        for a in range(2):
            for target in range(n_cp):
                near_copy(1, target, cp, a, u, flips[target % 2]).start()
            for target in range(n_cp):
                @pl.when(cp != target)
                def _():
                    near_copy(0, target, cp, a, u, vp).start()
            near_own(a, u).start()
        return 0

    lax.fori_loop(0, pieces, launch, 0)

    def wait_wanted(other, _):
        want_arrival(lax.rem(me + other, group)).wait_recv()
        return 0

    lax.fori_loop(1, group, wait_wanted, 0)

    band = lax.broadcasted_iota(jnp.int32, (2 * chip, wanted.shape[2]), 0)
    band = jnp.where(band < chip, vp * chip + band, peer_first * chip + band - chip)

    slot_rows = wanted.shape[2] // 2
    first_half = lax.broadcasted_iota(jnp.int32, (1, wanted.shape[2]), 1) < slot_rows
    for a in range(2):
        for j, of_chip in enumerate((peer_last, vp)):
            for c in range(0, n_cp, 2):
                device = of_chip * n_cp + c
                row = jnp.where(first_half, wanted[device][a : a + 1], wanted[device + 1][a : a + 1])
                hot = jnp.where(band == row, 1.0, 0.0).T
                at = (j * n_cp + c) * slot_rows
                chosen[a, pl.ds(at, 2 * slot_rows), :] = hot.astype(jnp.bfloat16)

    def pick(u):
        for a in range(2):
            found = jnp.dot(chosen[a], near[a, u], preferred_element_type=jnp.float32).astype(jnp.bfloat16)
            for j, put in enumerate((sent, picked)):
                for c in range(n_cp):
                    got_rows = found[(j * n_cp + c) * slot_rows : (j * n_cp + c + 1) * slot_rows]
                    if c == 0:
                        put[u, a, pl.ds(0, row_bands), :] = got_rows[:row_bands]
                    for p in range(groups):
                        put[u, a, pl.ds(row_bands + (p * n_cp + c) * pair_bands, pair_bands), :] = got_rows[
                            row_bands + p * pair_bands : row_bands + (p + 1) * pair_bands
                        ]

    lane = 256 if piece % 256 == 0 else 128

    def densities(start, p, with_rows):
        lanes = pl.ds(pl.multiple_of(start, lane), lane)
        val = ready[0, pl.ds(0, row_bands), lanes].astype(jnp.float32)
        cond = ready[1, pl.ds(0, row_bands), lanes].astype(jnp.float32)
        row_val = [spread(val[q * TV : (q + 1) * TV]) for q in range(ROW_TILES)]
        row_cond = [spread(cond[q * TC : (q + 1) * TC]) for q in range(ROW_TILES)]
        last = groups * rows
        if with_rows:
            for q in range(ROW_TILES):
                pair_rows(rho, last + q * block, row_val[q], twice(cond[q * TC : (q + 1) * TC]), lanes)
        span = pl.ds(pl.multiple_of(row_bands + p * pair_bands, 16), pair_bands)
        val = ready[0, span, lanes].astype(jnp.float32)
        cond = ready[1, span, lanes].astype(jnp.float32)
        for s in range(PAIR):
            slot_val, slot_cond = val[s * TV : (s + 1) * TV], cond[s * TC : (s + 1) * TC]
            right_val, right_cond = twice(slot_val), twice(slot_cond)
            at = pl.multiple_of(last + (ROW_TILES + p * PAIR + s) * block, block)
            pair_rows(rho, at, spread(slot_val), right_cond, lanes)
            first = pl.multiple_of(p * rows + 2 * ROW_TILES * s * block, block)
            for q in range(ROW_TILES):
                pair_rows(rho, first + q * block, row_val[q], right_val, lanes)
                pair_rows(rho, first + (ROW_TILES + q) * block, row_cond[q], right_cond, lanes)

    def hand_out(u, p):
        lanes = pl.ds(pl.multiple_of(cp * part + u * piece, 128), piece)
        for copy in cross_copies(u, p):
            copy.wait_recv()
        span = pl.ds(pl.multiple_of(row_bands + p * n_cp * pair_bands, 16), n_cp * pair_bands)
        mine = pl.ds(pl.multiple_of(row_bands + (p * n_cp + cp) * pair_bands, 16), pair_bands)
        home = pl.ds(pl.multiple_of(row_bands + p * pair_bands, 16), pair_bands)
        spans = [(span, mine, home)]
        if isinstance(p, int) and p == 0:
            tiles = pl.ds(0, row_bands)
            spans.append((tiles, tiles, tiles))
        for a in range(2):
            for span, mine, home in spans:
                total[u, a, span, :] = picked[u, a, span, :] + came[u, a, span, :]
                ready[a, home, lanes] = total[u, a, mine, :]
        for c in range(n_cp):
            @pl.when(cp != c)
            def _():
                for copy in give_copies(c, cp, u, p):
                    copy.start()

    def take_in(u, p):
        for c in range(n_cp):
            @pl.when(cp != c)
            def _():
                for copy in give_copies(c, c, u, p):
                    copy.wait_recv()

        def each(i, _):
            c, j = i // (piece // lane), lax.rem(i, piece // lane)
            densities(c * part + u * piece + j * lane, p, isinstance(p, int) and p == 0)
            return 0

        lax.fori_loop(0, n_cp * (piece // lane), each, 0)

    def flow(t, _):
        @pl.when(t < pieces)
        def _():
            for a in range(2):
                near_own(a, t).wait()
                for c in range(n_cp):
                    @pl.when(cp != c)
                    def _():
                        near_copy(0, c, c, a, t, vp).wait_recv()
                    near_copy(1, c, c, a, t, vp).wait_recv()
            pick(t)
            for copy in cross_copies(t, 0):
                copy.start()

            @pl.when(t == pieces - 1)
            def _():
                def later(i, _):
                    for copy in cross_copies(lax.rem(i, pieces), 1 + i // pieces):
                        copy.start()
                    return 0

                lax.fori_loop(0, pieces * (groups - 1), later, 0)

        @pl.when(jnp.logical_and(t >= 1, t <= pieces))
        def _():
            hand_out(t - 1, 0)

        @pl.when(t >= 2)
        def _():
            take_in(t - 2, 0)

        return 0

    lax.fori_loop(0, pieces + 2, flow, 0)

    depth = 1024
    toward = (-1, 1)

    def hop(way, k, h):
        return pltpu.make_async_remote_copy(
            src_ref=own.at[way, k, h],
            dst_ref=got.at[way, k, h],
            send_sem=send_sem.at[way, k, h],
            recv_sem=recv_sem.at[way, k, h],
            device_id={"ga": lax.rem(z + toward[way] + n, n)},
            device_id_type=pl.DeviceIdType.MESH,
        )

    far = (n - 1 - z, z)

    def step(i, _):
        @pl.when(i < steps)
        def _():
            first = pl.multiple_of((i // halves) * rows, rows)
            for way in range(2):
                column = pl.multiple_of((way * halves + lax.rem(i, halves)) * width, width)

                for c in range(halves):
                    @pl.when(i == c)
                    def _():
                        copies[way * halves + c].wait()

                acc[...] = jnp.zeros_like(acc)

                def deep(k, _):
                    at = pl.multiple_of(k * depth, depth)
                    acc[...] += jnp.dot(
                        rho[pl.ds(first, rows), pl.ds(at, depth)],
                        basis[pl.ds(at, depth), pl.ds(column, width)],
                        preferred_element_type=jnp.float32,
                    )
                    return 0

                lax.fori_loop(0, grid // depth, deep, 0)
                for h in range(QUARTERS):
                    own[way, i, h] = acc[pl.ds(h * (rows // QUARTERS), rows // QUARTERS), :].astype(jnp.bfloat16)

        for h in range(QUARTERS):
            for way in range(2):
                k = i - LAG * far[way]

                @pl.when(jnp.logical_and(k >= 0, k < steps))
                def _():
                    @pl.when(far[way] > 0)
                    def _():
                        hop(way, k, h).wait_recv()
                        summed = own[way, k, h].astype(jnp.float32) + got[way, k, h].astype(jnp.float32)
                        own[way, k, h] = summed.astype(jnp.bfloat16)

                    @pl.when(z != ends[way])
                    def _():
                        hop(way, k, h).start()

        for way in range(2):
            k = i - LAG * far[way]
            p = k // halves
            done = jnp.logical_and(k >= 0, jnp.logical_and(lax.rem(k, halves) == halves - 1, p < groups))

            @pl.when(jnp.logical_and(z == ends[way], done))
            def _():
                wide = ROW_TILES * block
                for s in range(PAIR):
                    direct = jnp.zeros((wide, wide), jnp.float32)
                    for c in range(halves):
                        weight = screen_ref[:, pl.ds((way * halves + c) * width, width)]
                        whole = own[way, p * halves + c].reshape(rows, width)
                        at = s * 2 * wide
                        direct += weighted_dot(whole[at : at + wide], weight, whole[at + wide : at + 2 * wide])
                    column = lax.broadcasted_iota(jnp.int32, (block, wide), 1)
                    dr_own[p * PAIR + s] = jnp.where(column < block, direct[:block], direct[block:])

        after = 1 + i // halves

        @pl.when(jnp.logical_and(after < groups, lax.rem(i, halves) == 0))
        def _():
            def out(u, _):
                hand_out(u, after)
                return 0

            lax.fori_loop(0, pieces, out, 0)

        @pl.when(jnp.logical_and(after < groups, lax.rem(i, halves) == halves - 1))
        def _():
            def into(u, _):
                take_in(u, after)
                return 0

            lax.fori_loop(0, pieces, into, 0)

        return 0

    lax.fori_loop(0, steps + LAG * (n - 1), step, 0)

    share = block // n

    def give(way, k):
        return [
            pltpu.make_async_remote_copy(
                src_ref=mine.at[k],
                dst_ref=there.at[way],
                send_sem=fin_send.at[k, j],
                recv_sem=fin_recv.at[way, j],
                device_id={"ga": k},
                device_id_type=pl.DeviceIdType.MESH,
            )
            for j, (mine, there) in enumerate(((ex_send, ex_got), (dr_send, dr_got)))
        ]

    for way in range(2):
        @pl.when(z == ends[way])
        def _():
            exchange = jnp.zeros(ex_own.shape, jnp.float32)
            for c in range(halves):
                weight = coulomb_ref[:, pl.ds((way * halves + c) * width, width)]
                whole = own[way, groups * halves + c].reshape(rows, width)
                left, right = whole[: ROW_TILES * block], whole[ROW_TILES * block :]
                exchange += weighted_dot(left, weight, right)
            ex_own[...] = exchange
            for k in range(n):
                if k != ends[way]:
                    for q in range(ROW_TILES):
                        ex_send[k, q] = ex_own[pl.ds(q * block + k * share, share), :].astype(jnp.bfloat16)
                    dr_send[k] = dr_own[:, pl.ds(k * share, share), :].astype(jnp.bfloat16)
                    for copy in give(way, k):
                        copy.start()
            for q in range(ROW_TILES):
                exch_ref[q] = ex_own[pl.ds(q * block + ends[way] * share, share), :]
            direct_ref[...] = dr_own[:, pl.ds(ends[way] * share, share), :]

    for way in range(2):
        @pl.when(z != ends[way])
        def _():
            for copy in give(way, 0):
                copy.wait_recv()
            here = ends[1 - way]

            def put(fresh):
                ex_part = ex_got[way].astype(jnp.float32)
                dr_part = dr_got[way].astype(jnp.float32)
                exch_ref[...] = ex_part if fresh else exch_ref[...] + ex_part
                direct_ref[...] = dr_part if fresh else direct_ref[...] + dr_part

            if way == 0:
                pl.when(z == here)(lambda: put(False))
                pl.when(z != here)(lambda: put(True))
            else:
                put(False)

    for way in range(2):
        @pl.when(z != ends[way])
        def _():
            def drain(k, _):
                for h in range(QUARTERS):
                    hop(way, k, h).wait_send()
                return 0

            lax.fori_loop(0, steps, drain, 0)

        @pl.when(z == ends[way])
        def _():
            for k in range(n):
                if k != ends[way]:
                    for copy in give(way, k):
                        copy.wait_send()

    for other in range(1, group):
        want_copy(lax.rem(me + other, group), other - 1).wait_send()

    def landed(u, _):
        for a in range(2):
            for target in range(n_cp):
                near_copy(1, target, cp, a, u, flips[target % 2]).wait_send()

                @pl.when(cp != target)
                def _():
                    near_copy(0, target, cp, a, u, vp).wait_send()
        for p in range(groups):
            for copy in cross_copies(u, p):
                copy.wait_send()
            for target in range(n_cp):
                @pl.when(cp != target)
                def _():
                    for copy in give_copies(target, cp, u, p):
                        copy.wait_send()
        return 0

    lax.fori_loop(0, pieces, landed, 0)


def make_tiles(sizes, slots, val, cond, wanted, basis, screen, coulomb):
    n, n_vp, n_cp = sizes
    grid, rank = basis.shape
    bands = val.shape[0]
    width = rank // 4
    block = TV * TC
    rows = (ROW_TILES + slots) * block
    total = (ROW_TILES + slots + 2 * ROW_TILES * slots) * block
    steps = (total // rows) * 2
    share = block // n
    part = grid // n_cp
    pieces = max(u for u in range(1, 5) if part % (u * 128) == 0)
    piece = part // pieces
    picked = (ROW_TILES + n_cp * slots) * TV
    vmem = pl.BlockSpec(memory_space=pltpu.VMEM)
    anywhere = pl.BlockSpec(memory_space=pl.ANY)
    bf16, f32 = jnp.bfloat16, jnp.float32
    return pl.pallas_call(
        functools.partial(tiles_kernel, n, n_vp, n_cp, slots),
        out_shape=(
            jax.ShapeDtypeStruct((ROW_TILES, share, slots * block), f32),
            jax.ShapeDtypeStruct((slots, share, ROW_TILES * block), f32),
        ),
        in_specs=[anywhere, anywhere, vmem, anywhere, vmem, vmem],
        out_specs=(vmem, vmem),
        scratch_shapes=[
            pltpu.VMEM((n_vp * n_cp,) + wanted.shape, jnp.int32),
            pltpu.VMEM((2, n_cp * wanted.shape[1], 2 * n_cp * bands), bf16),
            pltpu.VMEM((2, pieces, 2 * n_cp * bands, piece), bf16),
            pltpu.VMEM((pieces, 2, picked, piece), bf16),
            pltpu.VMEM((pieces, 2, picked, piece), bf16),
            pltpu.VMEM((pieces, 2, picked, piece), bf16),
            pltpu.VMEM((pieces, 2, picked, piece), bf16),
            pltpu.VMEM((2, (ROW_TILES + slots) * TV, grid), bf16),
            pltpu.VMEM((grid, rank), bf16),
            pltpu.VMEM((total, grid), bf16),
            pltpu.VMEM((rows, width), f32),
            pltpu.VMEM((2, steps, QUARTERS, rows // QUARTERS, width), bf16),
            pltpu.VMEM((2, steps, QUARTERS, rows // QUARTERS, width), bf16),
            pltpu.VMEM((ROW_TILES * block, slots * block), f32),
            pltpu.VMEM((slots, block, ROW_TILES * block), f32),
            pltpu.VMEM((n, ROW_TILES, share, slots * block), bf16),
            pltpu.VMEM((n, slots, share, ROW_TILES * block), bf16),
            pltpu.VMEM((2, ROW_TILES, share, slots * block), bf16),
            pltpu.VMEM((2, slots, share, ROW_TILES * block), bf16),
            pltpu.SemaphoreType.DMA((n_vp * n_cp,)),
            pltpu.SemaphoreType.DMA((n_vp * n_cp,)),
            pltpu.SemaphoreType.DMA((2, n_cp, 2, pieces)),
            pltpu.SemaphoreType.DMA((2, n_cp, 2, pieces)),
            pltpu.SemaphoreType.DMA((pieces, slots // PAIR)),
            pltpu.SemaphoreType.DMA((pieces, slots // PAIR)),
            pltpu.SemaphoreType.DMA((n_cp, pieces, slots // PAIR + 1)),
            pltpu.SemaphoreType.DMA((n_cp, pieces, slots // PAIR + 1)),
            pltpu.SemaphoreType.DMA((4,)),
            pltpu.SemaphoreType.DMA((2, steps, QUARTERS)),
            pltpu.SemaphoreType.DMA((2, steps, QUARTERS)),
            pltpu.SemaphoreType.DMA((n, 2)),
            pltpu.SemaphoreType.DMA((2, 2)),
        ],
        compiler_params=pltpu.CompilerParams(
            collective_id=0, has_side_effects=True, vmem_limit_bytes=67043328
        ),
    )(val, cond, wanted, basis, screen, coulomb)


def shards(valence_wavefunction, cond_wave, screen_basis, screen, coulomb, window_rows, tile_owner):
    slots = tile_owner.shape[0]
    n = lax.axis_size("ga")
    sizes = (n, lax.axis_size("vp"), lax.axis_size("cp"))
    pair_tiles = jnp.concatenate([window_rows, tile_owner])
    each = jnp.arange(TV, dtype=jnp.int32)[None, :]
    wanted = jnp.stack(
        [
            ((pair_tiles // NCT)[:, None] * TV + each).reshape(-1),
            ((pair_tiles % NCT)[:, None] * TC + each).reshape(-1),
        ]
    )
    wanted = jnp.pad(jnp.concatenate([wanted, wanted], axis=1), ((0, 6), (0, 0)), constant_values=-1)
    exchange, direct = make_tiles(
        sizes, slots, valence_wavefunction, cond_wave, wanted, screen_basis, screen[None], coulomb[None]
    )
    v = TV // n
    exchange = exchange.reshape(2, v, TC, slots, TV, TC).transpose(0, 3, 1, 2, 4, 5)
    direct = direct.reshape(slots, v, TV, 2, TC, TC).transpose(3, 0, 1, 4, 2, 5)
    kernel = (2.0 * exchange - direct).reshape(2, slots, -1)
    live = (tile_owner[None, :] >= window_rows[:, None])[:, :, None]
    return jnp.where(live, kernel, jnp.zeros_like(kernel))


def solution(mesh):
    in_specs = (
        P(("vp", "cp"), "ga"),
        P(("vp", "cp"), "ga"),
        P("ga", None),
        P(),
        P(),
        P(),
        P(("vp", "cp")),
    )
    out_specs = P(None, ("vp", "cp"), "ga")
    return jax.shard_map(shards, mesh=mesh, in_specs=in_specs, out_specs=out_specs, check_vma=False)
```

```python
import functools
import jax
import jax.numpy as jnp
from jax import lax
from jax.experimental import pallas as pl
from jax.experimental.pallas import tpu as pltpu
from jax.sharding import PartitionSpec as P

TV = 8
TC = 8
NCT = 64
LAG = 1
ROW_TILES = 2
PAIR = 2
QUARTERS = 8


def pair_rows(rho, first, left, right, lanes):
    for i in range(len(left)):
        rho[pl.ds(first + 16 * i, 16), lanes] = left[i] * right


def spread(tile):
    out = []
    for i in range(0, tile.shape[0], 2):
        two = [jnp.broadcast_to(tile[i + j : i + j + 1], (8, tile.shape[1])) for j in range(2)]
        out.append(jnp.concatenate(two, axis=0).astype(jnp.bfloat16))
    return out


def twice(tile):
    return jnp.concatenate([tile, tile], axis=0).astype(jnp.bfloat16)


def dot_t(a, b):
    return lax.dot_general(a, b, (((1,), (1,)), ((), ())), preferred_element_type=jnp.float32)


def weighted_dot(a, weight, b):
    scaled = a.astype(jnp.float32) * weight
    high = scaled.astype(jnp.bfloat16)
    low = (scaled - high.astype(jnp.float32)).astype(jnp.bfloat16)
    return dot_t(high, b) + dot_t(low, b)


def tiles_kernel(
    n, n_vp, n_cp, slots, val_hbm, cond_hbm, wanted_ref, basis_hbm, screen_ref, coulomb_ref,
    exch_ref, direct_ref, wanted, chosen, near, picked, sent, came, total, ready, basis, rho, acc, own, got, ex_own, dr_own, ex_send, dr_send, ex_got, dr_got,
    want_send, want_recv, near_send, near_recv, cross_send, cross_recv, give_send, give_recv,
    basis_sem, send_sem, recv_sem, fin_send, fin_recv,
):
    z = lax.axis_index("ga")
    grid, rank = basis_hbm.shape
    steps, quarters, quarter, width = own.shape[1:]
    rows = quarters * quarter
    halves = rank // (2 * width)
    ends = (0, n - 1)
    block = TV * TC

    copies = []
    for c in range(2 * halves):
        cols = pl.ds(c * width, width)
        copy = pltpu.make_async_copy(basis_hbm.at[:, cols], basis.at[:, cols], basis_sem.at[c])
        copy.start()
        copies.append(copy)

    barrier = pltpu.get_barrier_semaphore()
    for other in range(1, n):
        pl.semaphore_signal(
            barrier, inc=1, device_id={"ga": lax.rem(z + other, n)}, device_id_type=pl.DeviceIdType.MESH
        )

    vp, cp = lax.axis_index("vp"), lax.axis_index("cp")
    group = n_vp * n_cp
    me = vp * n_cp + cp
    for other in range(1, group):
        peer = lax.rem(me + other, group)
        pl.semaphore_signal(
            barrier, inc=1, device_id={"vp": peer // n_cp, "cp": lax.rem(peer, n_cp)},
            device_id_type=pl.DeviceIdType.MESH,
        )
    pl.semaphore_wait(barrier, n - 1 + group - 1)

    waves = (val_hbm, cond_hbm)
    bands = val_hbm.shape[0]
    chip = n_cp * bands
    part = grid // n_cp
    pieces = near_send.shape[-1]
    piece = part // pieces
    side = lax.rem(cp, 2)
    flips = (vp + 1 - 2 * lax.rem(vp, 2), lax.rem(vp + n_vp // 2, n_vp))
    peer_first = (1 - side) * flips[0] + side * flips[1]
    peer_last = (1 - side) * flips[1] + side * flips[0]

    def want_copy(peer, slot):
        return pltpu.make_async_remote_copy(
            src_ref=wanted_ref,
            dst_ref=wanted.at[me],
            send_sem=want_send.at[slot],
            recv_sem=want_recv.at[me],
            device_id={"vp": peer // n_cp, "cp": lax.rem(peer, n_cp)},
            device_id_type=pl.DeviceIdType.MESH,
        )

    def want_arrival(source):
        return pltpu.make_async_remote_copy(
            src_ref=wanted_ref,
            dst_ref=wanted.at[source],
            send_sem=want_send.at[0],
            recv_sem=want_recv.at[source],
            device_id={"vp": vp, "cp": cp},
            device_id_type=pl.DeviceIdType.MESH,
        )

    def near_copy(j, target, owner_cp, a, u, peer):
        return pltpu.make_async_remote_copy(
            src_ref=waves[a].at[:, pl.ds(pl.multiple_of(target * part + u * piece, 128), piece)],
            dst_ref=near.at[a, u, pl.ds(pl.multiple_of(j * chip + owner_cp * bands, bands), bands), :],
            send_sem=near_send.at[j, target, a, u],
            recv_sem=near_recv.at[j, owner_cp, a, u],
            device_id={"vp": peer, "cp": target},
            device_id_type=pl.DeviceIdType.MESH,
        )

    def near_own(a, u):
        return pltpu.make_async_copy(
            waves[a].at[:, pl.ds(pl.multiple_of(cp * part + u * piece, 128), piece)],
            near.at[a, u, pl.ds(pl.multiple_of(cp * bands, bands), bands), :],
            near_recv.at[0, cp, a, u],
        )

    row_bands = ROW_TILES * TV
    pair_bands = PAIR * TV
    groups = slots // PAIR

    def cross_copies(u, p):
        spans = [pl.ds(pl.multiple_of(row_bands + p * n_cp * pair_bands, 16), n_cp * pair_bands)]
        if isinstance(p, int) and p == 0:
            spans = [pl.ds(0, row_bands + n_cp * pair_bands)]
        return [
            pltpu.make_async_remote_copy(
                src_ref=sent.at[u, :, span, :],
                dst_ref=came.at[u, :, span, :],
                send_sem=cross_send.at[u, p],
                recv_sem=cross_recv.at[u, p],
                device_id={"vp": peer_last, "cp": cp},
                device_id_type=pl.DeviceIdType.MESH,
            )
            for span in spans
        ]

    def give_copies(target, source_cp, u, p):
        lanes = pl.ds(pl.multiple_of(source_cp * part + u * piece, 128), piece)
        spans = [
            (
                pl.ds(pl.multiple_of(row_bands + (p * n_cp + target) * pair_bands, 16), pair_bands),
                pl.ds(pl.multiple_of(row_bands + p * pair_bands, 16), pair_bands),
                p,
            )
        ]
        if isinstance(p, int) and p == 0:
            spans.append((pl.ds(0, row_bands), pl.ds(0, row_bands), groups))
        return [
            pltpu.make_async_remote_copy(
                src_ref=total.at[u, :, src, :],
                dst_ref=ready.at[:, dst, lanes],
                send_sem=give_send.at[target, u, j],
                recv_sem=give_recv.at[source_cp, u, j],
                device_id={"vp": vp, "cp": target},
                device_id_type=pl.DeviceIdType.MESH,
            )
            for src, dst, j in spans
        ]

    for other in range(1, group):
        want_copy(lax.rem(me + other, group), other - 1).start()
    wanted[me] = wanted_ref[...]

    def launch(u, _):
        for a in range(2):
            for target in range(n_cp):
                near_copy(1, target, cp, a, u, flips[target % 2]).start()
            for target in range(n_cp):
                @pl.when(cp != target)
                def _():
                    near_copy(0, target, cp, a, u, vp).start()
            near_own(a, u).start()
        return 0

    lax.fori_loop(0, pieces, launch, 0)

    def wait_wanted(other, _):
        want_arrival(lax.rem(me + other, group)).wait_recv()
        return 0

    lax.fori_loop(1, group, wait_wanted, 0)

    band = lax.broadcasted_iota(jnp.int32, (2 * chip, wanted.shape[2]), 0)
    band = jnp.where(band < chip, vp * chip + band, peer_first * chip + band - chip)

    slot_rows = wanted.shape[2] // 2
    first_half = lax.broadcasted_iota(jnp.int32, (1, wanted.shape[2]), 1) < slot_rows
    for a in range(2):
        for j, of_chip in enumerate((peer_last, vp)):
            for c in range(0, n_cp, 2):
                device = of_chip * n_cp + c
                row = jnp.where(first_half, wanted[device][a : a + 1], wanted[device + 1][a : a + 1])
                hot = jnp.where(band == row, 1.0, 0.0).T
                at = (j * n_cp + c) * slot_rows
                chosen[a, pl.ds(at, 2 * slot_rows), :] = hot.astype(jnp.bfloat16)

    def pick(u):
        for a in range(2):
            found = jnp.dot(chosen[a], near[a, u], preferred_element_type=jnp.float32).astype(jnp.bfloat16)
            for j, put in enumerate((sent, picked)):
                for c in range(n_cp):
                    got_rows = found[(j * n_cp + c) * slot_rows : (j * n_cp + c + 1) * slot_rows]
                    if c == 0:
                        put[u, a, pl.ds(0, row_bands), :] = got_rows[:row_bands]
                    for p in range(groups):
                        put[u, a, pl.ds(row_bands + (p * n_cp + c) * pair_bands, pair_bands), :] = got_rows[
                            row_bands + p * pair_bands : row_bands + (p + 1) * pair_bands
                        ]

    lane = 256 if piece % 256 == 0 else 128

    def densities(start, p, with_rows):
        lanes = pl.ds(pl.multiple_of(start, lane), lane)
        val = ready[0, pl.ds(0, row_bands), lanes].astype(jnp.float32)
        cond = ready[1, pl.ds(0, row_bands), lanes].astype(jnp.float32)
        row_val = [spread(val[q * TV : (q + 1) * TV]) for q in range(ROW_TILES)]
        row_cond = [spread(cond[q * TC : (q + 1) * TC]) for q in range(ROW_TILES)]
        last = groups * rows
        if with_rows:
            for q in range(ROW_TILES):
                pair_rows(rho, last + q * block, row_val[q], twice(cond[q * TC : (q + 1) * TC]), lanes)
        span = pl.ds(pl.multiple_of(row_bands + p * pair_bands, 16), pair_bands)
        val = ready[0, span, lanes].astype(jnp.float32)
        cond = ready[1, span, lanes].astype(jnp.float32)
        for s in range(PAIR):
            slot_val, slot_cond = val[s * TV : (s + 1) * TV], cond[s * TC : (s + 1) * TC]
            right_val, right_cond = twice(slot_val), twice(slot_cond)
            at = pl.multiple_of(last + (ROW_TILES + p * PAIR + s) * block, block)
            pair_rows(rho, at, spread(slot_val), right_cond, lanes)
            first = pl.multiple_of(p * rows + 2 * ROW_TILES * s * block, block)
            for q in range(ROW_TILES):
                pair_rows(rho, first + q * block, row_val[q], right_val, lanes)
                pair_rows(rho, first + (ROW_TILES + q) * block, row_cond[q], right_cond, lanes)

    def hand_out(u, p):
        lanes = pl.ds(pl.multiple_of(cp * part + u * piece, 128), piece)
        for copy in cross_copies(u, p):
            copy.wait_recv()
        span = pl.ds(pl.multiple_of(row_bands + p * n_cp * pair_bands, 16), n_cp * pair_bands)
        mine = pl.ds(pl.multiple_of(row_bands + (p * n_cp + cp) * pair_bands, 16), pair_bands)
        home = pl.ds(pl.multiple_of(row_bands + p * pair_bands, 16), pair_bands)
        spans = [(span, mine, home)]
        if isinstance(p, int) and p == 0:
            tiles = pl.ds(0, row_bands)
            spans.append((tiles, tiles, tiles))
        for a in range(2):
            for span, mine, home in spans:
                total[u, a, span, :] = picked[u, a, span, :] + came[u, a, span, :]
                ready[a, home, lanes] = total[u, a, mine, :]
        for c in range(n_cp):
            @pl.when(cp != c)
            def _():
                for copy in give_copies(c, cp, u, p):
                    copy.start()

    def take_in(u, p):
        for c in range(n_cp):
            @pl.when(cp != c)
            def _():
                for copy in give_copies(c, c, u, p):
                    copy.wait_recv()

        def each(i, _):
            c, j = i // (piece // lane), lax.rem(i, piece // lane)
            densities(c * part + u * piece + j * lane, p, isinstance(p, int) and p == 0)
            return 0

        lax.fori_loop(0, n_cp * (piece // lane), each, 0)

    def flow(t, _):
        @pl.when(t < pieces)
        def _():
            for a in range(2):
                near_own(a, t).wait()
                for c in range(n_cp):
                    @pl.when(cp != c)
                    def _():
                        near_copy(0, c, c, a, t, vp).wait_recv()
                    near_copy(1, c, c, a, t, vp).wait_recv()
            pick(t)
            for copy in cross_copies(t, 0):
                copy.start()

            @pl.when(t == pieces - 1)
            def _():
                def later(i, _):
                    for copy in cross_copies(lax.rem(i, pieces), 1 + i // pieces):
                        copy.start()
                    return 0

                lax.fori_loop(0, pieces * (groups - 1), later, 0)

        @pl.when(jnp.logical_and(t >= 1, t <= pieces))
        def _():
            hand_out(t - 1, 0)

        @pl.when(t >= 2)
        def _():
            take_in(t - 2, 0)

        return 0

    lax.fori_loop(0, pieces + 2, flow, 0)

    depth = 1024
    toward = (-1, 1)

    def hop(way, k, h):
        return pltpu.make_async_remote_copy(
            src_ref=own.at[way, k, h],
            dst_ref=got.at[way, k, h],
            send_sem=send_sem.at[way, k, h],
            recv_sem=recv_sem.at[way, k, h],
            device_id={"ga": lax.rem(z + toward[way] + n, n)},
            device_id_type=pl.DeviceIdType.MESH,
        )

    far = (n - 1 - z, z)

    def relay(i, way, h):
        k = i - LAG * far[way]

        @pl.when(jnp.logical_and(k >= 0, k < steps))
        def _():
            @pl.when(far[way] > 0)
            def _():
                hop(way, k, h).wait_recv()
                summed = own[way, k, h].astype(jnp.float32) + got[way, k, h].astype(jnp.float32)
                own[way, k, h] = summed.astype(jnp.bfloat16)

            @pl.when(z != ends[way])
            def _():
                hop(way, k, h).start()

    def step(i, _):
        @pl.when(i < steps)
        def _():
            first = pl.multiple_of((i // halves) * rows, rows)
            for way in range(2):
                column = pl.multiple_of((way * halves + lax.rem(i, halves)) * width, width)

                for c in range(halves):
                    @pl.when(i == c)
                    def _():
                        copies[way * halves + c].wait()

                acc[...] = jnp.zeros_like(acc)

                def deep(k, _):
                    at = pl.multiple_of(k * depth, depth)
                    acc[...] += jnp.dot(
                        rho[pl.ds(first, rows), pl.ds(at, depth)],
                        basis[pl.ds(at, depth), pl.ds(column, width)],
                        preferred_element_type=jnp.float32,
                    )
                    return 0

                lax.fori_loop(0, grid // depth, deep, 0)
                for h in range(QUARTERS):
                    own[way, i, h] = acc[pl.ds(h * (rows // QUARTERS), rows // QUARTERS), :].astype(jnp.bfloat16)
                if way == 0:
                    for h in range(QUARTERS):
                        relay(i, 0, h)

        @pl.when(i < steps)
        def _():
            for h in range(QUARTERS):
                relay(i, 1, h)

        @pl.when(i >= steps)
        def _():
            for h in range(QUARTERS):
                for way in range(2):
                    relay(i, way, h)

        for way in range(2):
            k = i - LAG * far[way]
            p = k // halves
            done = jnp.logical_and(k >= 0, jnp.logical_and(lax.rem(k, halves) == halves - 1, p < groups))

            @pl.when(jnp.logical_and(z == ends[way], done))
            def _():
                wide = ROW_TILES * block
                for s in range(PAIR):
                    direct = jnp.zeros((wide, wide), jnp.float32)
                    for c in range(halves):
                        weight = screen_ref[:, pl.ds((way * halves + c) * width, width)]
                        whole = own[way, p * halves + c].reshape(rows, width)
                        at = s * 2 * wide
                        direct += weighted_dot(whole[at : at + wide], weight, whole[at + wide : at + 2 * wide])
                    column = lax.broadcasted_iota(jnp.int32, (block, wide), 1)
                    dr_own[p * PAIR + s] = jnp.where(column < block, direct[:block], direct[block:])

        after = 1 + i // halves

        @pl.when(jnp.logical_and(after < groups, lax.rem(i, halves) == 0))
        def _():
            def out(u, _):
                hand_out(u, after)
                return 0

            lax.fori_loop(0, pieces, out, 0)

        @pl.when(jnp.logical_and(after < groups, lax.rem(i, halves) == halves - 1))
        def _():
            def into(u, _):
                take_in(u, after)
                return 0

            lax.fori_loop(0, pieces, into, 0)

        return 0

    lax.fori_loop(0, steps + LAG * (n - 1), step, 0)

    share = block // n

    def give(way, k):
        return [
            pltpu.make_async_remote_copy(
                src_ref=mine.at[k],
                dst_ref=there.at[way],
                send_sem=fin_send.at[k, j],
                recv_sem=fin_recv.at[way, j],
                device_id={"ga": k},
                device_id_type=pl.DeviceIdType.MESH,
            )
            for j, (mine, there) in enumerate(((ex_send, ex_got), (dr_send, dr_got)))
        ]

    for way in range(2):
        @pl.when(z == ends[way])
        def _():
            exchange = jnp.zeros(ex_own.shape, jnp.float32)
            for c in range(halves):
                weight = coulomb_ref[:, pl.ds((way * halves + c) * width, width)]
                whole = own[way, groups * halves + c].reshape(rows, width)
                left, right = whole[: ROW_TILES * block], whole[ROW_TILES * block :]
                exchange += weighted_dot(left, weight, right)
            ex_own[...] = exchange
            for k in range(n):
                if k != ends[way]:
                    for q in range(ROW_TILES):
                        ex_send[k, q] = ex_own[pl.ds(q * block + k * share, share), :].astype(jnp.bfloat16)
                    dr_send[k] = dr_own[:, pl.ds(k * share, share), :].astype(jnp.bfloat16)
                    for copy in give(way, k):
                        copy.start()
            for q in range(ROW_TILES):
                exch_ref[q] = ex_own[pl.ds(q * block + ends[way] * share, share), :]
            direct_ref[...] = dr_own[:, pl.ds(ends[way] * share, share), :]

    for way in range(2):
        @pl.when(z != ends[way])
        def _():
            for copy in give(way, 0):
                copy.wait_recv()
            here = ends[1 - way]

            def put(fresh):
                ex_part = ex_got[way].astype(jnp.float32)
                dr_part = dr_got[way].astype(jnp.float32)
                exch_ref[...] = ex_part if fresh else exch_ref[...] + ex_part
                direct_ref[...] = dr_part if fresh else direct_ref[...] + dr_part

            if way == 0:
                pl.when(z == here)(lambda: put(False))
                pl.when(z != here)(lambda: put(True))
            else:
                put(False)

    for way in range(2):
        @pl.when(z != ends[way])
        def _():
            def drain(k, _):
                for h in range(QUARTERS):
                    hop(way, k, h).wait_send()
                return 0

            lax.fori_loop(0, steps, drain, 0)

        @pl.when(z == ends[way])
        def _():
            for k in range(n):
                if k != ends[way]:
                    for copy in give(way, k):
                        copy.wait_send()

    for other in range(1, group):
        want_copy(lax.rem(me + other, group), other - 1).wait_send()

    def landed(u, _):
        for a in range(2):
            for target in range(n_cp):
                near_copy(1, target, cp, a, u, flips[target % 2]).wait_send()

                @pl.when(cp != target)
                def _():
                    near_copy(0, target, cp, a, u, vp).wait_send()
        for p in range(groups):
            for copy in cross_copies(u, p):
                copy.wait_send()
            for target in range(n_cp):
                @pl.when(cp != target)
                def _():
                    for copy in give_copies(target, cp, u, p):
                        copy.wait_send()
        return 0

    lax.fori_loop(0, pieces, landed, 0)


def make_tiles(sizes, slots, val, cond, wanted, basis, screen, coulomb):
    n, n_vp, n_cp = sizes
    grid, rank = basis.shape
    bands = val.shape[0]
    width = rank // 4
    block = TV * TC
    rows = (ROW_TILES + slots) * block
    total = (ROW_TILES + slots + 2 * ROW_TILES * slots) * block
    steps = (total // rows) * 2
    share = block // n
    part = grid // n_cp
    pieces = max(u for u in range(1, 5) if part % (u * 128) == 0)
    piece = part // pieces
    picked = (ROW_TILES + n_cp * slots) * TV
    vmem = pl.BlockSpec(memory_space=pltpu.VMEM)
    anywhere = pl.BlockSpec(memory_space=pl.ANY)
    bf16, f32 = jnp.bfloat16, jnp.float32
    return pl.pallas_call(
        functools.partial(tiles_kernel, n, n_vp, n_cp, slots),
        out_shape=(
            jax.ShapeDtypeStruct((ROW_TILES, share, slots * block), f32),
            jax.ShapeDtypeStruct((slots, share, ROW_TILES * block), f32),
        ),
        in_specs=[anywhere, anywhere, vmem, anywhere, vmem, vmem],
        out_specs=(vmem, vmem),
        scratch_shapes=[
            pltpu.VMEM((n_vp * n_cp,) + wanted.shape, jnp.int32),
            pltpu.VMEM((2, n_cp * wanted.shape[1], 2 * n_cp * bands), bf16),
            pltpu.VMEM((2, pieces, 2 * n_cp * bands, piece), bf16),
            pltpu.VMEM((pieces, 2, picked, piece), bf16),
            pltpu.VMEM((pieces, 2, picked, piece), bf16),
            pltpu.VMEM((pieces, 2, picked, piece), bf16),
            pltpu.VMEM((pieces, 2, picked, piece), bf16),
            pltpu.VMEM((2, (ROW_TILES + slots) * TV, grid), bf16),
            pltpu.VMEM((grid, rank), bf16),
            pltpu.VMEM((total, grid), bf16),
            pltpu.VMEM((rows, width), f32),
            pltpu.VMEM((2, steps, QUARTERS, rows // QUARTERS, width), bf16),
            pltpu.VMEM((2, steps, QUARTERS, rows // QUARTERS, width), bf16),
            pltpu.VMEM((ROW_TILES * block, slots * block), f32),
            pltpu.VMEM((slots, block, ROW_TILES * block), f32),
            pltpu.VMEM((n, ROW_TILES, share, slots * block), bf16),
            pltpu.VMEM((n, slots, share, ROW_TILES * block), bf16),
            pltpu.VMEM((2, ROW_TILES, share, slots * block), bf16),
            pltpu.VMEM((2, slots, share, ROW_TILES * block), bf16),
            pltpu.SemaphoreType.DMA((n_vp * n_cp,)),
            pltpu.SemaphoreType.DMA((n_vp * n_cp,)),
            pltpu.SemaphoreType.DMA((2, n_cp, 2, pieces)),
            pltpu.SemaphoreType.DMA((2, n_cp, 2, pieces)),
            pltpu.SemaphoreType.DMA((pieces, slots // PAIR)),
            pltpu.SemaphoreType.DMA((pieces, slots // PAIR)),
            pltpu.SemaphoreType.DMA((n_cp, pieces, slots // PAIR + 1)),
            pltpu.SemaphoreType.DMA((n_cp, pieces, slots // PAIR + 1)),
            pltpu.SemaphoreType.DMA((4,)),
            pltpu.SemaphoreType.DMA((2, steps, QUARTERS)),
            pltpu.SemaphoreType.DMA((2, steps, QUARTERS)),
            pltpu.SemaphoreType.DMA((n, 2)),
            pltpu.SemaphoreType.DMA((2, 2)),
        ],
        compiler_params=pltpu.CompilerParams(
            collective_id=0, has_side_effects=True, vmem_limit_bytes=67043328
        ),
    )(val, cond, wanted, basis, screen, coulomb)


def shards(valence_wavefunction, cond_wave, screen_basis, screen, coulomb, window_rows, tile_owner):
    slots = tile_owner.shape[0]
    n = lax.axis_size("ga")
    sizes = (n, lax.axis_size("vp"), lax.axis_size("cp"))
    pair_tiles = jnp.concatenate([window_rows, tile_owner])
    each = jnp.arange(TV, dtype=jnp.int32)[None, :]
    wanted = jnp.stack(
        [
            ((pair_tiles // NCT)[:, None] * TV + each).reshape(-1),
            ((pair_tiles % NCT)[:, None] * TC + each).reshape(-1),
        ]
    )
    wanted = jnp.pad(jnp.concatenate([wanted, wanted], axis=1), ((0, 6), (0, 0)), constant_values=-1)
    exchange, direct = make_tiles(
        sizes, slots, valence_wavefunction, cond_wave, wanted, screen_basis, screen[None], coulomb[None]
    )
    v = TV // n
    exchange = exchange.reshape(2, v, TC, slots, TV, TC).transpose(0, 3, 1, 2, 4, 5)
    direct = direct.reshape(slots, v, TV, 2, TC, TC).transpose(3, 0, 1, 4, 2, 5)
    kernel = (2.0 * exchange - direct).reshape(2, slots, -1)
    live = (tile_owner[None, :] >= window_rows[:, None])[:, :, None]
    return jnp.where(live, kernel, jnp.zeros_like(kernel))


def solution(mesh):
    in_specs = (
        P(("vp", "cp"), "ga"),
        P(("vp", "cp"), "ga"),
        P("ga", None),
        P(),
        P(),
        P(),
        P(("vp", "cp")),
    )
    out_specs = P(None, ("vp", "cp"), "ga")
    return jax.shard_map(shards, mesh=mesh, in_specs=in_specs, out_specs=out_specs, check_vma=False)
```
